128 devices in a mesh: site: 8 (over z, core), bond: 16 (over y, x).
Axes of the slice: x: 4, y: 4, z: 4, core: 2. Of those that a mesh axis runs over, the one named last changes fastest.
Arguments:
- left_env: float32 [8, 512, 16, 512], P('site', 'bond'), may hold values from -6 to 6
- right_env: float32 [8, 512, 16, 512], P('site', 'bond'), may hold values from -6 to 6
- left_site: float32 [8, 512, 4, 512], P('site'), may hold values from -0.125 to 0.125
- right_site: float32 [8, 512, 4, 512], P('site'), may hold values from -0.125 to 0.125
- left_mpo: float32 [8, 16, 16, 4, 4], P('site'), may hold values from -1.5 to 1.5
- right_mpo: float32 [8, 16, 16, 4, 4], P('site'), may hold values from -1.5 to 1.5
Outputs:
- new_left: float32 [8, 512, 16, 512], P('site', 'bond')
- new_right: float32 [8, 512, 16, 512], P('site', 'bond')
The draws below stay inside these ranges and needn't reach their ends.
All inputs are finite; a program needn't handle non-finite values.
Results may differ from the reference program's by a relative error of at most 0.0001.
Values sent between devices are 32-bit elements; how exact they have to be, the bound alone decides.
A program may use at most 128 MiB of HBM per device.

```python
import jax
import jax.numpy as jnp
from jax import lax

D = 512
W = 16
PHYS = 4
SEGS = 8


def levels(stream_key, dims, split, low, top_value):
    factor_of = 1.0
    for axis_at, shards_of in split:
        heights = jax.random.uniform(jax.random.fold_in(jax.random.fold_in(stream_key, 6), axis_at), (shards_of,), jnp.float32, low / len(split), top_value / len(split))
        factor_of = factor_of * jnp.repeat(jnp.exp(heights), dims[axis_at] // shards_of).reshape((-1,) + (1,) * (len(dims) - 1 - axis_at))
    return factor_of


def bell_draw(key, extent, scale, reach, cuts=(), kind=jnp.bfloat16):
    factor_of = levels(key, extent, cuts, -0.22, 0.18) if cuts else 1.0
    array = jax.random.normal(key, extent, jnp.float32) * scale * factor_of
    return jnp.minimum(jnp.maximum(array, -reach), reach).astype(kind)


def setup_inputs(seed: int = 0) -> dict:
    seeds = jax.random.split(jax.random.key(seed), 7)
    left_env = bell_draw(seeds[0], (SEGS, D, W, D), 1.0, 6.0, ((0, 8), (1, 16)), jnp.float32)
    right_env = bell_draw(seeds[1], (SEGS, D, W, D), 1.0, 6.0, ((0, 8), (1, 16)), jnp.float32)
    left_site = bell_draw(seeds[2], (SEGS, D, PHYS, D), (D * PHYS) ** -0.5, 0.125, ((0, 8),), jnp.float32)
    right_site = bell_draw(seeds[3], (SEGS, D, PHYS, D), (D * PHYS) ** -0.5, 0.125, ((0, 8),), jnp.float32)
    left_mpo = bell_draw(seeds[4], (SEGS, W, W, PHYS, PHYS), W ** -0.5, 1.5, ((0, 8),), jnp.float32)
    right_mpo = bell_draw(seeds[5], (SEGS, W, W, PHYS, PHYS), W ** -0.5, 1.5, ((0, 8),), jnp.float32)
    return dict(left_env=left_env, right_env=right_env, left_site=left_site, right_site=right_site, left_mpo=left_mpo, right_mpo=right_mpo)


def grow_env(environ, tensor, operator):
    first_part = jnp.einsum("awc,asb->wcsb", environ, tensor, precision=lax.Precision.HIGHEST)
    second_part = jnp.einsum("wcsb,wvst->bvct", first_part, operator, precision=lax.Precision.HIGHEST)
    result = jnp.dot(second_part.reshape(D * W, D * PHYS), tensor.reshape(D * PHYS, D), precision=lax.Precision.HIGHEST)
    return result.reshape(D, W, D)


def reference(left_env, right_env, left_site, right_site, left_mpo, right_mpo):
    grown_left = []
    grown_right = []
    for segment in range(SEGS):
        grown_left.append(grow_env(left_env[segment], left_site[segment], left_mpo[segment]))
        grown_right.append(grow_env(right_env[segment], right_site[segment], jnp.transpose(right_mpo[segment], (1, 0, 2, 3))))
    new_left = jnp.stack([left_env[0]] + grown_left[:-1])
    new_right = jnp.stack(grown_right[1:] + [right_env[SEGS - 1]])
    return new_left, new_right
```

```python
import jax
import jax.numpy as jnp
from jax import lax
from jax.experimental import pallas as pl
from jax.experimental.pallas import tpu as pltpu
from jax.sharding import PartitionSpec as P

MESH = pl.DeviceIdType.MESH
F32 = jnp.float32
BF16 = jnp.bfloat16


def split(value):
    high = value.astype(BF16)
    return high, (value - high.astype(F32)).astype(BF16)


def dot3(ah, al, bh, bl):
    out = jnp.dot(ah, bh, preferred_element_type=F32)
    out += jnp.dot(ah, bl, preferred_element_type=F32)
    out += jnp.dot(al, bh, preferred_element_type=F32)
    return out


def kernel(
    le, re, ls, rs, mm, nl, nr,
    buf, a1f, a2f, bdf, a1h, a1l, a2h, a2l, bdh, bdl, qh, ql, part, rcv,
    rsem, xsem, ysem, ssem, a1sem, a2sem, bdsem, a1snd, a2snd, bdsnd,
    prcv, psnd, orcv, osnd,
):
    site = lax.axis_index("site")
    bond = lax.axis_index("bond")
    z, core = site // 2, site % 2
    y, x = bond // 4, bond % 4
    sib = 1 - core
    side = x // 2
    owner = core == x % 2
    e_half = 256 * (y % 2)

    def dev(zz, cc, yy, xx):
        return (2 * zz + cc, 4 * yy + xx)

    up, down, far = (y + 1) % 4, (y + 3) % 4, (y + 2) % 4

    barrier = pltpu.get_barrier_semaphore()

    def greet(n, c):
        zz = (z + n // 8) % 4
        cc, xx = (core + (n % 8) // 4) % 2, (x + n % 4) % 4
        pl.semaphore_signal(barrier, inc=1, device_id=dev(zz, cc, y, xx), device_id_type=MESH)
        return c

    lax.fori_loop(1, 16, greet, 0)
    lax.fori_loop(24, 32, greet, 0)
    for yy in (up, down, far):
        pl.semaphore_signal(barrier, inc=1, device_id=dev(z, core, yy, x), device_id_type=MESH)
    pl.semaphore_wait(barrier, 26)

    def x_copy(sd, h):
        env = (le, re)[sd]
        return pltpu.make_async_remote_copy(
            src_ref=env.at[0, pl.ds(16 * h, 16)],
            dst_ref=buf.at[4 * h + x],
            send_sem=xsem.at[2 * sd + h],
            recv_sem=rsem.at[4 * h + x],
            device_id=dev(z, h, y, 2 * sd + core),
            device_id_type=MESH,
        )

    def is_local(sd, h):
        return (2 * sd + core == x) & (core == h)

    for sd in (0, 1):
        for h in (0, 1):
            env = (le, re)[sd]

            @pl.when(is_local(sd, h))
            def _():
                pltpu.make_async_copy(
                    env.at[0, pl.ds(16 * h, 16)], buf.at[4 * h + x], rsem.at[4 * h + x]
                ).start()

            @pl.when(jnp.logical_not(is_local(sd, h)))
            def _():
                x_copy(sd, h).start()

    def row_of(slot):
        grp, xx = slot // 4, slot % 4
        yy = (y + grp // 2 + 2 * (grp // 3)) % 4
        return 128 * yy + 32 * xx + 16 * (grp % 2)

    def a1_src(t_site, t, c):
        return t_site.at[0, :, t, pl.ds(pl.multiple_of(e_half + 128 * c, 128), 128)]

    def a1_copy(t_site, t):
        return pltpu.make_async_remote_copy(
            src_ref=a1_src(t_site, t, sib), dst_ref=a1f.at[t],
            send_sem=a1snd.at[t], recv_sem=a1sem.at[t],
            device_id=dev(z, sib, y, x), device_id_type=MESH,
        )

    def a2_copy(t_site, slot):
        return pltpu.make_async_remote_copy(
            src_ref=t_site.at[0, pl.ds(row_of(slot), 16)], dst_ref=a2f.at[slot],
            send_sem=a2snd.at[slot], recv_sem=a2sem.at[slot],
            device_id=dev(z, sib, y, x), device_id_type=MESH,
        )

    def bd_copy(sd):
        return pltpu.make_async_remote_copy(
            src_ref=mm.at[sd], dst_ref=bdf, send_sem=bdsnd, recv_sem=bdsem,
            device_id=dev(z, sib, y, x), device_id_type=MESH,
        )

    for sd in (0, 1):
        t_site = (ls, rs)[sd]

        @pl.when(owner & (side == sd))
        def _():
            for t in range(4):
                pltpu.make_async_copy(a1_src(t_site, t, core), a1f.at[t], a1sem.at[t]).start()
                a1_copy(t_site, t).start()
            pltpu.make_async_copy(mm.at[sd], bdf, bdsem).start()
            bd_copy(sd).start()

            def rows(slot, c):
                pltpu.make_async_copy(
                    t_site.at[0, pl.ds(row_of(slot), 16)], a2f.at[slot], a2sem.at[slot]
                ).start()
                a2_copy(t_site, slot).start()
                return c

            lax.fori_loop(0, 16, rows, 0)

    def block_wait(slot):
        pltpu.make_async_copy(buf.at[slot], buf.at[slot], rsem.at[slot]).wait()

    def to_sib(slot, n):
        return pltpu.make_async_remote_copy(
            src_ref=buf.at[slot], dst_ref=buf.at[slot],
            send_sem=ssem.at[n], recv_sem=rsem.at[slot],
            device_id=dev(z, sib, y, x), device_id_type=MESH,
        )

    def to_row(xx, n):
        return pltpu.make_async_remote_copy(
            src_ref=buf.at[4 * core + xx], dst_ref=buf.at[8 + 4 * core + xx],
            send_sem=ysem.at[n], recv_sem=rsem.at[8 + 4 * core + xx],
            device_id=dev(z, core, (y + 3 + 2 * core) % 4, x), device_id_type=MESH,
        )

    def col_of(i):
        return (x + i + i // 2 - 2 * (i // 3)) % 4

    for t in range(4):
        pltpu.make_async_copy(a1f.at[t], a1f.at[t], a1sem.at[t]).wait()
        a1h[:, 128 * t : 128 * (t + 1)], a1l[:, 128 * t : 128 * (t + 1)] = split(a1f[t])
    pltpu.make_async_copy(bdf, bdf, bdsem).wait()
    bdh[...], bdl[...] = split(bdf[...])

    def turn(n, c):
        for k in (0, 1):
            pltpu.make_async_copy(
                a2f.at[2 * n + k], a2f.at[2 * n + k], a2sem.at[2 * n + k]
            ).wait()
        rows = jnp.concatenate([a2f[2 * n].reshape(64, 512), a2f[2 * n + 1].reshape(64, 512)], axis=0)
        high, low = split(jnp.transpose(rows))
        a2h[:, pl.ds(pl.multiple_of(128 * n, 128), 128)] = high
        a2l[:, pl.ds(pl.multiple_of(128 * n, 128), 128)] = low
        return c

    def first_two(slot):
        lh, ll = split(buf[slot].reshape(256, 512))
        ph, pw = split(dot3(lh, ll, a1h[...], a1l[...]))

        def stack(p):
            return jnp.concatenate(
                [
                    jnp.concatenate(
                        [
                            p[64 * g + 16 * j : 64 * g + 16 * j + 16, 128 * t : 128 * t + 128]
                            for j in range(4)
                            for t in range(4)
                        ],
                        axis=0,
                    )
                    for g in range(4)
                ],
                axis=1,
            )

        oh, ol = split(dot3(bdh[...], bdl[...], stack(ph), stack(pw)))
        for g in range(4):
            at = pl.ds(pl.multiple_of(64 * slot + 16 * g, 16), 16)
            for v in range(16):
                rows, cols = slice(16 * v, 16 * v + 16), slice(128 * g, 128 * g + 128)
                qh[at, 128 * v : 128 * v + 128] = oh[rows, cols]
                ql[at, 128 * v : 128 * v + 128] = ol[rows, cols]

    def step(n, c):
        kind = n % 4
        i = n // 4 - (kind + 1) // 2

        @pl.when((i >= 0) & (i < 4))
        def _():
            xx = col_of(i)
            from_sib = kind // 2
            grp = (1 - from_sib) * (core + 2 * kind) + from_sib * (sib + 2 * (kind - 2))
            slot = 4 * grp + xx
            block_wait(slot)

            @pl.when(kind == 0)
            def _():
                to_row(xx, i).start()

            @pl.when(kind < 2)
            def _():
                to_sib(slot, 4 * kind + i).start()

            first_two(slot)

        @pl.when(n == 0)
        def _():
            lax.fori_loop(0, 8, turn, 0)

        return c

    lax.fori_loop(0, 24, step, 0)

    def last(n, row):
        lhs = pl.ds(pl.multiple_of(128 * row, 128), 128)
        flat = part.reshape(4, 2048, 128)

        def cols(i, c):
            at = pl.ds(pl.multiple_of(256 * i, 256), 256)
            out = dot3(a2h[lhs, :], a2l[lhs, :], qh[:, at], ql[:, at])
            for k in (0, 1):
                flat[n, pl.ds(2 * i + k, 128, stride=16), :] = out[:, 128 * k : 128 * k + 128]
            return c

        lax.fori_loop(0, 8, cols, 0)

    def part_copy(n, row):
        return pltpu.make_async_remote_copy(
            src_ref=part.at[n], dst_ref=rcv.at[n],
            send_sem=psnd.at[n], recv_sem=prcv.at[n],
            device_id=dev(z, core, row, x), device_id_type=MESH,
        )

    targets = (far, up, down)
    for n, row in enumerate(targets):
        last(n, row)
        part_copy(n, row).start()
    last(3, y)

    segment = 2 * z + x % 2
    target = segment + 1 - 2 * side
    valid = (target >= 0) & (target < 8)

    def out_copy(sd, n, xx):
        src = (part.at[3], rcv.at[1])[n]
        half = (y % 2) if n == 0 else 1 - y % 2
        lanes = pl.ds(pl.multiple_of(256 * half + 128 * core, 128), 128)
        out = (nl, nr)[sd]
        return pltpu.make_async_remote_copy(
            src_ref=src.at[pl.ds(32 * xx, 32)], dst_ref=out.at[0, :, :, lanes],
            send_sem=osnd.at[4 * n + xx], recv_sem=orcv.at[4 * sd + 2 * n + core],
            device_id=(target, 4 * y + xx), device_id_type=MESH,
        )

    def out_local(sd, n):
        src = (part.at[3], rcv.at[1])[n]
        half = (y % 2) if n == 0 else 1 - y % 2
        lanes = pl.ds(pl.multiple_of(256 * half + 128 * core, 128), 128)
        out = (nl, nr)[sd]
        return pltpu.make_async_copy(
            src.at[pl.ds(32 * x, 32)], out.at[0, :, :, lanes], orcv.at[4 * sd + 2 * n + core]
        )

    def hand_off(n, wait):
        for sd in (0, 1):

            @pl.when(valid & (side == sd))
            def _():
                def one(d, c):
                    xx = (x + d) % 4
                    local = (d == 0) & (target == site)

                    @pl.when(jnp.logical_not(local))
                    def _():
                        if wait:
                            out_copy(sd, n, xx).wait_send()
                        else:
                            out_copy(sd, n, xx).start()

                    if not wait:

                        @pl.when(local)
                        def _():
                            out_local(sd, n).start()

                    return c

                lax.fori_loop(0, 4, one, 0)

    part_copy(1, up).wait_recv()
    part_copy(2, down).wait_recv()

    def add_one(i, c):
        at = pl.ds(8 * i, 8)
        rcv[1, at] = rcv[1, at] + rcv[2, at]
        return c

    lax.fori_loop(0, 16, add_one, 0)
    hand_off(1, False)
    part_copy(0, far).wait_recv()

    def add_zero(i, c):
        at = pl.ds(8 * i, 8)
        part[3, at] = part[3, at] + rcv[0, at]
        return c

    lax.fori_loop(0, 16, add_zero, 0)
    hand_off(0, False)

    for sd in (0, 1):
        for h in (0, 1):

            @pl.when(jnp.logical_not(is_local(sd, h)))
            def _():
                x_copy(sd, h).wait_send()

    for i in range(4):
        to_row(col_of(i), i).wait_send()
        to_sib(4 * core + col_of(i), i).wait_send()
        to_sib(8 + 4 * core + col_of(i), 4 + i).wait_send()
    for sd in (0, 1):
        t_site = (ls, rs)[sd]

        @pl.when(owner & (side == sd))
        def _():
            for t in range(4):
                a1_copy(t_site, t).wait_send()
            bd_copy(sd).wait_send()

            def rows(slot, c):
                a2_copy(t_site, slot).wait_send()
                return c

            lax.fori_loop(0, 16, rows, 0)

    for n, row in enumerate(targets):
        part_copy(n, row).wait_send()
    hand_off(1, True)
    hand_off(0, True)
    for sd in (0, 1):

        @pl.when((site > 0) if sd == 0 else (site < 7))
        def _():
            out = (nl, nr)[sd]
            for k in range(4):
                block = out.at[0, :, :, pl.ds(128 * k, 128)]
                pltpu.make_async_copy(block, block, orcv.at[4 * sd + k]).wait()


def grow(left_env, right_env, left_site, right_site, operators):
    any_space = pl.BlockSpec(memory_space=pl.ANY)
    dma = pltpu.SemaphoreType.DMA
    vmem = pltpu.VMEM
    return pl.pallas_call(
        kernel,
        out_shape=[jax.ShapeDtypeStruct(left_env.shape, F32)] * 2,
        in_specs=[any_space] * 5,
        out_specs=[any_space] * 2,
        scratch_shapes=[
            vmem((16, 16, 16, 512), F32),
            vmem((4, 512, 128), F32),
            vmem((16, 16, 4, 512), F32),
            vmem((256, 256), F32),
            vmem((512, 512), BF16),
            vmem((512, 512), BF16),
            vmem((512, 1024), BF16),
            vmem((512, 1024), BF16),
            vmem((256, 256), BF16),
            vmem((256, 256), BF16),
            vmem((1024, 2048), BF16),
            vmem((1024, 2048), BF16),
            vmem((4, 128, 16, 128), F32),
            vmem((3, 128, 16, 128), F32),
            dma((16,)), dma((4,)), dma((4,)), dma((8,)),
            dma((4,)), dma((16,)), dma, dma((4,)), dma((16,)), dma,
            dma((3,)), dma((3,)), dma((8,)), dma((8,)),
        ],
        compiler_params=pltpu.CompilerParams(
            collective_id=0, has_side_effects=True, vmem_limit_bytes=62 * 1024 * 1024
        ),
    )(left_env, right_env, left_site, right_site, operators)


def spread(operator):
    states = operator.shape[2]
    width = operator.shape[0]
    same = jnp.eye(states, dtype=jnp.bool_)[None, :, None, :, None, None]
    whole = jnp.where(same, operator.transpose(1, 2, 3, 0)[:, None, :, None], 0.0)
    return whole.reshape(width * states * states, width * states * states)


def local(left_env, right_env, left_site, right_site, left_mpo, right_mpo):
    operators = jnp.stack(
        [spread(left_mpo[0]), spread(jnp.transpose(right_mpo[0], (1, 0, 2, 3)))]
    )
    from_left, from_right = grow(left_env, right_env, left_site, right_site, operators)
    segment = lax.axis_index("site")
    last_segment = lax.axis_size("site") - 1
    new_left = jnp.where(segment == 0, left_env, from_left)
    new_right = jnp.where(segment == last_segment, right_env, from_right)
    return (new_left, new_right)


def solution(mesh):
    return jax.shard_map(
        local,
        mesh=mesh,
        in_specs=(
            P("site", "bond", None, None),
            P("site", "bond", None, None),
            P("site", None, None, None),
            P("site", None, None, None),
            P("site", None, None, None, None),
            P("site", None, None, None, None),
        ),
        out_specs=(P("site", "bond", None, None), P("site", "bond", None, None)),
        check_vma=False,
    )
```

```python
import jax
import jax.numpy as jnp
from jax import lax
from jax.experimental import pallas as pl
from jax.experimental.pallas import tpu as pltpu
from jax.sharding import PartitionSpec as P

MESH = pl.DeviceIdType.MESH
F32 = jnp.float32
BF16 = jnp.bfloat16
DELAY = 1


def split(value):
    high = value.astype(BF16)
    return high, (value - high.astype(F32)).astype(BF16)


def dot3(ah, al, bh, bl):
    out = jnp.dot(ah, bh, preferred_element_type=F32)
    out += jnp.dot(ah, bl, preferred_element_type=F32)
    out += jnp.dot(al, bh, preferred_element_type=F32)
    return out


def kernel(
    le, re, ls, rs, lm, rm, nl, nr,
    buf, a1f, a2f, mpo, a1h, a1l, a2h, a2l, bdh, bdl, qh, ql, part, rcv, kept,
    rsem, xrcv, xsem, ysem, ssem, a1sem, a2sem, mposem, a1snd, a2snd, mposnd,
    prcv, psnd, orcv, osnd, ksem,
):
    site = lax.axis_index("site")
    bond = lax.axis_index("bond")
    z, core = site // 2, site % 2
    y, x = bond // 4, bond % 4
    sib = 1 - core
    side = x // 2
    owner = core == x % 2
    e_half = 256 * (y % 2)

    def dev(zz, cc, yy, xx):
        return (2 * zz + cc, 4 * yy + xx)

    up, down, far = (y + 1) % 4, (y + 3) % 4, (y + 2) % 4

    barrier = pltpu.get_barrier_semaphore()

    def greet(n, c):
        zz = (z + n // 8) % 4
        cc, xx = (core + (n % 8) // 4) % 2, (x + n % 4) % 4
        pl.semaphore_signal(barrier, inc=1, device_id=dev(zz, cc, y, xx), device_id_type=MESH)
        return c

    lax.fori_loop(1, 16, greet, 0)
    lax.fori_loop(24, 32, greet, 0)
    for yy in (up, down, far):
        pl.semaphore_signal(barrier, inc=1, device_id=dev(z, core, yy, x), device_id_type=MESH)
    pl.semaphore_wait(barrier, 26)

    def x_copy(sd, h, lo, count, sem):
        env = (le, re)[sd]
        return pltpu.make_async_remote_copy(
            src_ref=env.at[0, pl.ds(16 * h + lo, count)],
            dst_ref=buf.at[4 * h + x, pl.ds(lo, count)],
            send_sem=xsem.at[2 * sd + h],
            recv_sem=xrcv.at[x, sem],
            device_id=dev(z, h, y, 2 * sd + core),
            device_id_type=MESH,
        )

    def hops(sd):
        return (2 * sd + core + 4 - x) % 4

    def pieces(sd):
        for k in range(4):
            for h in (0, 1):
                x_copy(sd, h, 4 * k, 4, k).start()

    for sd in (0, 1):

        @pl.when(hops(sd) % 2 == 1)
        def _():
            pieces(sd)

        @pl.when(hops(sd) == 0)
        def _():
            for h in (0, 1):

                @pl.when(core == h)
                def _():
                    pltpu.make_async_copy(
                        (le, re)[sd].at[0, pl.ds(16 * h, 16)], buf.at[4 * h + x], xrcv.at[x, 0]
                    ).start()

                @pl.when(core != h)
                def _():
                    x_copy(sd, h, 0, 16, 0).start()

    keeps = (site == 0, site == 7)
    for sd in (0, 1):

        @pl.when(keeps[sd])
        def _():
            pltpu.make_async_copy((le, re)[sd].at[0], kept, ksem).start()

    def row_of(slot):
        grp, xx = slot // 4, slot % 4
        yy = (y + grp // 2 + 2 * (grp // 3)) % 4
        return 128 * yy + 32 * xx + 16 * (grp % 2)

    def a1_src(t_site, t, c):
        return t_site.at[0, :, t, pl.ds(pl.multiple_of(e_half + 128 * c, 128), 128)]

    def a1_copy(t_site, t):
        return pltpu.make_async_remote_copy(
            src_ref=a1_src(t_site, t, sib), dst_ref=a1f.at[t],
            send_sem=a1snd.at[t], recv_sem=a1sem.at[t],
            device_id=dev(z, sib, y, x), device_id_type=MESH,
        )

    def a2_copy(t_site, slot):
        return pltpu.make_async_remote_copy(
            src_ref=t_site.at[0, pl.ds(row_of(slot), 16)], dst_ref=a2f.at[slot],
            send_sem=a2snd.at[slot], recv_sem=a2sem.at[slot],
            device_id=dev(z, sib, y, x), device_id_type=MESH,
        )

    def mpo_copy(sd):
        return pltpu.make_async_remote_copy(
            src_ref=(lm, rm)[sd], dst_ref=mpo, send_sem=mposnd, recv_sem=mposem,
            device_id=dev(z, sib, y, x), device_id_type=MESH,
        )

    for sd in (0, 1):
        t_site = (ls, rs)[sd]

        @pl.when(owner & (side == sd))
        def _():
            for t in range(4):
                pltpu.make_async_copy(a1_src(t_site, t, core), a1f.at[t], a1sem.at[t]).start()
                a1_copy(t_site, t).start()
            pltpu.make_async_copy((lm, rm)[sd], mpo, mposem).start()
            mpo_copy(sd).start()

            def rows(slot, c):
                pltpu.make_async_copy(
                    t_site.at[0, pl.ds(row_of(slot), 16)], a2f.at[slot], a2sem.at[slot]
                ).start()
                a2_copy(t_site, slot).start()
                return c

            lax.fori_loop(0, 16, rows, 0)

    def block_wait(slot):
        pltpu.make_async_copy(buf.at[slot], buf.at[slot], rsem.at[slot]).wait()

    def to_sib(slot, n):
        return pltpu.make_async_remote_copy(
            src_ref=buf.at[slot], dst_ref=buf.at[slot],
            send_sem=ssem.at[n], recv_sem=rsem.at[slot],
            device_id=dev(z, sib, y, x), device_id_type=MESH,
        )

    def to_row(xx, lo, count):
        return pltpu.make_async_remote_copy(
            src_ref=buf.at[4 * core + xx, pl.ds(lo, count)],
            dst_ref=buf.at[8 + 4 * core + xx, pl.ds(lo, count)],
            send_sem=ysem.at[xx], recv_sem=rsem.at[8 + 4 * core + xx],
            device_id=dev(z, core, (y + 3 + 2 * core) % 4, x), device_id_type=MESH,
        )

    def x_wait(xx, lo, count, sem):
        at = buf.at[4 * core + xx, pl.ds(lo, count)]
        pltpu.make_async_copy(at, at, xrcv.at[xx, sem]).wait()

    def col_of(i):
        return (x + i + i // 2 - 2 * (i // 3)) % 4

    x_wait(x, 0, 16, 0)
    to_row(x, 0, 16).start()
    to_sib(4 * core + x, 0).start()

    pltpu.make_async_copy(mpo, mpo, mposem).wait()
    small = split(mpo[...].reshape(256, 16))
    row = lax.broadcasted_iota(jnp.int32, (256, 256), 0)
    col = lax.broadcasted_iota(jnp.int32, (256, 256), 1)
    diagonal = ((row >> 2) & 3) == (col >> 6)

    def ones(mask):
        return jnp.where(mask, 1.0, 0.0).astype(BF16)

    @pl.when(side == 0)
    def _():
        pick = ones((lax.broadcasted_iota(jnp.int32, (256, 16), 0) >> 4)
                    == lax.broadcasted_iota(jnp.int32, (256, 16), 1))
        move = ones(((row >> 4) == (col & 15)) & ((row & 3) == ((col >> 4) & 3)))
        for value, ref in zip(small, (bdh, bdl)):
            wide = lax.dot_general(pick, value, (((1,), (1,)), ((), ())), preferred_element_type=F32)
            wide = jnp.where(((col >> 2) & 3) == (row & 3), wide, 0.0).astype(BF16)
            out = jnp.dot(wide, move, preferred_element_type=F32)
            ref[...] = jnp.where(diagonal, out, 0.0).astype(BF16)

    @pl.when(side == 1)
    def _():
        pick = ones((lax.broadcasted_iota(jnp.int32, (16, 256), 1) & 15)
                    == lax.broadcasted_iota(jnp.int32, (16, 256), 0))
        move = ones(((col >> 4) == (row >> 4)) & (((col >> 2) & 3) == (row & 3)))
        for value, ref in zip(small, (bdh, bdl)):
            wide = jnp.dot(value, pick, preferred_element_type=F32)
            wide = jnp.where((row & 3) == ((col >> 4) & 3), wide, 0.0).astype(BF16)
            out = jnp.dot(move, wide, preferred_element_type=F32)
            ref[...] = jnp.where(diagonal, out, 0.0).astype(BF16)

    for t in range(4):
        pltpu.make_async_copy(a1f.at[t], a1f.at[t], a1sem.at[t]).wait()
        a1h[:, 128 * t : 128 * (t + 1)], a1l[:, 128 * t : 128 * (t + 1)] = split(a1f[t])

    def turn(n, c):
        for k in (0, 1):
            pltpu.make_async_copy(
                a2f.at[2 * n + k], a2f.at[2 * n + k], a2sem.at[2 * n + k]
            ).wait()
        rows = jnp.concatenate([a2f[2 * n].reshape(64, 512), a2f[2 * n + 1].reshape(64, 512)], axis=0)
        high, low = split(jnp.transpose(rows))
        a2h[:, pl.ds(pl.multiple_of(128 * n, 128), 128)] = high
        a2l[:, pl.ds(pl.multiple_of(128 * n, 128), 128)] = low
        return c

    def first_two(slot):
        lh, ll = split(buf[slot].reshape(256, 512))
        ph, pw = split(dot3(lh, ll, a1h[...], a1l[...]))

        def stack(p):
            return jnp.concatenate(
                [
                    jnp.concatenate(
                        [
                            p[64 * g + 16 * j : 64 * g + 16 * j + 16, 128 * t : 128 * t + 128]
                            for j in range(4)
                            for t in range(4)
                        ],
                        axis=0,
                    )
                    for g in range(4)
                ],
                axis=1,
            )

        oh, ol = split(dot3(bdh[...], bdl[...], stack(ph), stack(pw)))
        for g in range(4):
            at = pl.ds(pl.multiple_of(64 * slot + 16 * g, 16), 16)
            for v in range(16):
                rows, cols = slice(16 * v, 16 * v + 16), slice(128 * g, 128 * g + 128)
                qh[at, 128 * v : 128 * v + 128] = oh[rows, cols]
                ql[at, 128 * v : 128 * v + 128] = ol[rows, cols]

    def step(n, c):
        kind = n % 4
        i = n // 4 - (kind + 1) // 2

        @pl.when((i >= 0) & (i < 4))
        def _():
            xx = col_of(i)
            from_sib = kind // 2
            grp = (1 - from_sib) * (core + 2 * kind) + from_sib * (sib + 2 * (kind - 2))
            slot = 4 * grp + xx

            @pl.when((kind == 0) & (i > 0))
            def _():
                for k in range(4):
                    x_wait(xx, 4 * k, 4, k)
                    to_row(xx, 4 * k, 4).start()
                    if k == DELAY:

                        @pl.when(i == 1)
                        def _():
                            for sd in (0, 1):

                                @pl.when(hops(sd) == 2)
                                def _():
                                    pieces(sd)

            @pl.when(kind > 0)
            def _():
                block_wait(slot)

            @pl.when((kind == 1) | ((kind == 0) & (i > 0)))
            def _():
                to_sib(slot, 4 * kind + i).start()

            first_two(slot)

        @pl.when(n == 0)
        def _():
            lax.fori_loop(0, 8, turn, 0)

        return c

    lax.fori_loop(0, 24, step, 0)

    def last(n, row):
        lhs = pl.ds(pl.multiple_of(128 * row, 128), 128)
        flat = part.reshape(4, 2048, 128)

        def cols(i, c):
            at = pl.ds(pl.multiple_of(256 * i, 256), 256)
            out = dot3(a2h[lhs, :], a2l[lhs, :], qh[:, at], ql[:, at])
            for k in (0, 1):
                flat[n, pl.ds(2 * i + k, 128, stride=16), :] = out[:, 128 * k : 128 * k + 128]
            return c

        lax.fori_loop(0, 8, cols, 0)

    def part_copy(n, row, i):
        at = pl.ds(32 * end_of(i), 32)
        return pltpu.make_async_remote_copy(
            src_ref=part.at[n, at], dst_ref=rcv.at[n, at],
            send_sem=psnd.at[n, i], recv_sem=prcv.at[n, i],
            device_id=dev(z, core, row, x), device_id_type=MESH,
        )

    def end_of(i):
        return (x + 2 + i + i // 2 - 2 * (i // 3)) % 4

    targets = (far, up, down)
    for n, row in enumerate(targets):
        last(n, row)
        for i in range(4):
            part_copy(n, row, i).start()
    last(3, y)

    segment = 2 * z + x % 2
    target = segment + 1 - 2 * side
    valid = (target >= 0) & (target < 8)

    def out_copy(sd, n, xx):
        src = (part.at[3], rcv.at[1])[n]
        half = (y % 2) if n == 0 else 1 - y % 2
        lanes = pl.ds(pl.multiple_of(256 * half + 128 * core, 128), 128)
        out = (nl, nr)[sd]
        return pltpu.make_async_remote_copy(
            src_ref=src.at[pl.ds(32 * xx, 32)], dst_ref=out.at[0, :, :, lanes],
            send_sem=osnd.at[4 * n + xx], recv_sem=orcv.at[4 * sd + 2 * n + core],
            device_id=(target, 4 * y + xx), device_id_type=MESH,
        )

    def out_local(sd, n):
        src = (part.at[3], rcv.at[1])[n]
        half = (y % 2) if n == 0 else 1 - y % 2
        lanes = pl.ds(pl.multiple_of(256 * half + 128 * core, 128), 128)
        out = (nl, nr)[sd]
        return pltpu.make_async_copy(
            src.at[pl.ds(32 * x, 32)], out.at[0, :, :, lanes], orcv.at[4 * sd + 2 * n + core]
        )

    def hand_off(n, xx, wait):
        local = (xx == x) & (target == site)
        for sd in (0, 1):

            @pl.when(valid & (side == sd))
            def _():
                @pl.when(jnp.logical_not(local))
                def _():
                    if wait:
                        out_copy(sd, n, xx).wait_send()
                    else:
                        out_copy(sd, n, xx).start()

                if not wait:

                    @pl.when(local)
                    def _():
                        out_local(sd, n).start()

    for sd in (0, 1):

        @pl.when(keeps[sd])
        def _():
            pltpu.make_async_copy((le, re)[sd].at[0], kept, ksem).wait()
            pltpu.make_async_copy(kept, (nl, nr)[sd].at[0], ksem).start()

    def finish(n, xx):
        def add(k, c):
            at = pl.ds(32 * xx + 8 * k, 8)
            if n == 0:
                part[3, at] = part[3, at] + rcv[0, at]
            else:
                rcv[1, at] = rcv[1, at] + rcv[2, at]
            return c

        lax.fori_loop(0, 4, add, 0)
        hand_off(n, xx, False)

    for i in range(4):
        part_copy(0, far, i).wait_recv()
        finish(0, end_of(i))
    for i in range(4):
        part_copy(1, up, i).wait_recv()
        part_copy(2, down, i).wait_recv()
        finish(1, end_of(i))

    for sd in (0, 1):
        for h in (0, 1):

            @pl.when((hops(sd) != 0) | (core != h))
            def _():
                x_copy(sd, h, 0, 16, 0).wait_send()

    for i in range(4):
        to_row(col_of(i), 0, 16).wait_send()
        to_sib(4 * core + col_of(i), i).wait_send()
        to_sib(8 + 4 * core + col_of(i), 4 + i).wait_send()
    for sd in (0, 1):
        t_site = (ls, rs)[sd]

        @pl.when(owner & (side == sd))
        def _():
            for t in range(4):
                a1_copy(t_site, t).wait_send()
            mpo_copy(sd).wait_send()

            def rows(slot, c):
                a2_copy(t_site, slot).wait_send()
                return c

            lax.fori_loop(0, 16, rows, 0)

    for n, row in enumerate(targets):
        for i in range(4):
            part_copy(n, row, i).wait_send()
    for i in range(4):
        for n in (0, 1):
            hand_off(n, end_of(i), True)
    for sd in (0, 1):

        @pl.when((site > 0) if sd == 0 else (site < 7))
        def _():
            out = (nl, nr)[sd]
            for k in range(4):
                block = out.at[0, :, :, pl.ds(128 * k, 128)]
                pltpu.make_async_copy(block, block, orcv.at[4 * sd + k]).wait()

        @pl.when(keeps[sd])
        def _():
            pltpu.make_async_copy(kept, (nl, nr)[sd].at[0], ksem).wait()


def grow(left_env, right_env, left_site, right_site, left_mpo, right_mpo):
    any_space = pl.BlockSpec(memory_space=pl.ANY)
    dma = pltpu.SemaphoreType.DMA
    vmem = pltpu.VMEM
    return pl.pallas_call(
        kernel,
        out_shape=[jax.ShapeDtypeStruct(left_env.shape, F32)] * 2,
        in_specs=[any_space] * 6,
        out_specs=[any_space] * 2,
        scratch_shapes=[
            vmem((16, 16, 16, 512), F32),
            vmem((4, 512, 128), F32),
            vmem((16, 16, 4, 512), F32),
            vmem((16, 4, 4, 16), F32),
            vmem((512, 512), BF16),
            vmem((512, 512), BF16),
            vmem((512, 1024), BF16),
            vmem((512, 1024), BF16),
            vmem((256, 256), BF16),
            vmem((256, 256), BF16),
            vmem((1024, 2048), BF16),
            vmem((1024, 2048), BF16),
            vmem((4, 128, 16, 128), F32),
            vmem((3, 128, 16, 128), F32),
            vmem((32, 16, 512), F32),
            dma((16,)), dma((4, 4)), dma((4,)), dma((4,)), dma((8,)),
            dma((4,)), dma((16,)), dma, dma((4,)), dma((16,)), dma,
            dma((3, 4)), dma((3, 4)), dma((8,)), dma((8,)), dma,
        ],
        compiler_params=pltpu.CompilerParams(
            collective_id=0, has_side_effects=True, vmem_limit_bytes=62 * 1024 * 1024
        ),
    )(left_env, right_env, left_site, right_site, left_mpo, right_mpo)


def local(left_env, right_env, left_site, right_site, left_mpo, right_mpo):
    def turned(operator):
        return jnp.transpose(operator[0], (0, 2, 3, 1))

    return tuple(
        grow(left_env, right_env, left_site, right_site, turned(left_mpo), turned(right_mpo))
    )


def solution(mesh):
    return jax.shard_map(
        local,
        mesh=mesh,
        in_specs=(
            P("site", "bond", None, None),
            P("site", "bond", None, None),
            P("site", None, None, None),
            P("site", None, None, None),
            P("site", None, None, None, None),
            P("site", None, None, None, None),
        ),
        out_specs=(P("site", "bond", None, None), P("site", "bond", None, None)),
        check_vma=False,
    )
```

```python
import jax
import jax.numpy as jnp
from jax import lax
from jax.experimental import pallas as pl
from jax.experimental.pallas import tpu as pltpu
from jax.sharding import PartitionSpec as P

MESH = pl.DeviceIdType.MESH
F32 = jnp.float32
BF16 = jnp.bfloat16


def split(value):
    high = value.astype(BF16)
    return high, (value - high.astype(F32)).astype(BF16)


def dot3(ah, al, bh, bl):
    out = jnp.dot(ah, bh, preferred_element_type=F32)
    out += jnp.dot(ah, bl, preferred_element_type=F32)
    out += jnp.dot(al, bh, preferred_element_type=F32)
    return out


def kernel(
    le, re, ls, rs, lm, rm, nl, nr,
    buf, a1f, a2f, mpo, a1h, a1l, a2h, a2l, bdh, bdl, qh, ql, part, rcv, kept,
    rsem, xrcv, xsem, ysem, ssem, a1sem, a2sem, mposem, a1snd, a2snd, mposnd,
    prcv, psnd, orcv, osnd, ksem, near,
):
    site = lax.axis_index("site")
    bond = lax.axis_index("bond")
    z, core = site // 2, site % 2
    y, x = bond // 4, bond % 4
    sib = 1 - core
    side = x // 2
    owner = core == x % 2
    e_half = 256 * (y % 2)

    def dev(zz, cc, yy, xx):
        return (2 * zz + cc, 4 * yy + xx)

    up, down, far = (y + 1) % 4, (y + 3) % 4, (y + 2) % 4

    barrier = pltpu.get_barrier_semaphore()

    def greet(n, c):
        there = dev(z, (core + n // 4) % 2, y, (x + n % 4) % 4)
        pl.semaphore_signal(barrier, inc=1, device_id=there, device_id_type=MESH)
        return c

    lax.fori_loop(1, 8, greet, 0)
    for yy in (up, down, far):
        pl.semaphore_signal(barrier, inc=1, device_id=dev(z, core, yy, x), device_id_type=MESH)
    above, below = z < 3, z > 0
    for there, step in ((above, 1), (below, -1)):

        @pl.when(there)
        def _():
            for cc in (0, 1):
                pl.semaphore_signal(
                    barrier, inc=1, device_id=dev(z + step, cc, y, x), device_id_type=MESH
                )

    pl.semaphore_wait(barrier, 10 + 2 * jnp.where(above, 1, 0) + 2 * jnp.where(below, 1, 0))

    def x_copy(sd, h, lo, count, sem):
        env = (le, re)[sd]
        return pltpu.make_async_remote_copy(
            src_ref=env.at[0, pl.ds(16 * h + lo, count)],
            dst_ref=buf.at[4 * h + x, pl.ds(lo, count)],
            send_sem=xsem.at[2 * sd + h],
            recv_sem=xrcv.at[x, sem],
            device_id=dev(z, h, y, 2 * sd + core),
            device_id_type=MESH,
        )

    def hops(sd):
        return (2 * sd + core + 4 - x) % 4

    def pieces(sd):
        for k in range(4):
            for h in (0, 1):
                x_copy(sd, h, 4 * k, 4, k).start()

    for sd in (0, 1):

        @pl.when(hops(sd) % 2 == 1)
        def _():
            pieces(sd)

        @pl.when(hops(sd) == 0)
        def _():
            for h in (0, 1):

                @pl.when(core == h)
                def _():
                    pltpu.make_async_copy(
                        (le, re)[sd].at[0, pl.ds(16 * h, 16)], buf.at[4 * h + x], xrcv.at[x, 0]
                    ).start()

                @pl.when(core != h)
                def _():
                    x_copy(sd, h, 0, 16, 0).start()

    def tell(n, c):
        there = dev(z, (core + n // 4) % 2, y, (x + n % 4) % 4)
        pl.semaphore_signal(near, inc=1, device_id=there, device_id_type=MESH)
        return c

    lax.fori_loop(1, 8, tell, 0)

    keeps = (site == 0, site == 7)
    for sd in (0, 1):

        @pl.when(keeps[sd])
        def _():
            pltpu.make_async_copy((le, re)[sd].at[0], kept, ksem).start()

    def row_of(slot):
        grp, xx = slot // 4, slot % 4
        yy = (y + grp // 2 + 2 * (grp // 3)) % 4
        return 128 * yy + 32 * xx + 16 * (grp % 2)

    def a1_src(t_site, t, c):
        return t_site.at[0, :, t, pl.ds(pl.multiple_of(e_half + 128 * c, 128), 128)]

    def a1_copy(t_site, t):
        return pltpu.make_async_remote_copy(
            src_ref=a1_src(t_site, t, sib), dst_ref=a1f.at[t],
            send_sem=a1snd.at[t], recv_sem=a1sem.at[t],
            device_id=dev(z, sib, y, x), device_id_type=MESH,
        )

    def a2_copy(t_site, slot):
        return pltpu.make_async_remote_copy(
            src_ref=t_site.at[0, pl.ds(row_of(slot), 16)], dst_ref=a2f.at[slot],
            send_sem=a2snd.at[slot], recv_sem=a2sem.at[slot],
            device_id=dev(z, sib, y, x), device_id_type=MESH,
        )

    def mpo_copy(sd):
        return pltpu.make_async_remote_copy(
            src_ref=(lm, rm)[sd], dst_ref=mpo, send_sem=mposnd, recv_sem=mposem,
            device_id=dev(z, sib, y, x), device_id_type=MESH,
        )

    for sd in (0, 1):
        t_site = (ls, rs)[sd]

        @pl.when(owner & (side == sd))
        def _():
            for t in range(4):
                pltpu.make_async_copy(a1_src(t_site, t, core), a1f.at[t], a1sem.at[t]).start()
                a1_copy(t_site, t).start()
            pltpu.make_async_copy((lm, rm)[sd], mpo, mposem).start()
            mpo_copy(sd).start()

    def block_wait(slot):
        pltpu.make_async_copy(buf.at[slot], buf.at[slot], rsem.at[slot]).wait()

    def to_sib(slot, n):
        return pltpu.make_async_remote_copy(
            src_ref=buf.at[slot], dst_ref=buf.at[slot],
            send_sem=ssem.at[n], recv_sem=rsem.at[slot],
            device_id=dev(z, sib, y, x), device_id_type=MESH,
        )

    def to_row(xx, lo, count):
        return pltpu.make_async_remote_copy(
            src_ref=buf.at[4 * core + xx, pl.ds(lo, count)],
            dst_ref=buf.at[8 + 4 * core + xx, pl.ds(lo, count)],
            send_sem=ysem.at[xx], recv_sem=rsem.at[8 + 4 * core + xx],
            device_id=dev(z, core, (y + 3 + 2 * core) % 4, x), device_id_type=MESH,
        )

    def x_wait(xx, lo, count, sem):
        at = buf.at[4 * core + xx, pl.ds(lo, count)]
        pltpu.make_async_copy(at, at, xrcv.at[xx, sem]).wait()

    def col_of(i):
        return (x + i + i // 2 - 2 * (i // 3)) % 4

    x_wait(x, 0, 16, 0)
    to_row(x, 0, 16).start()
    to_sib(4 * core + x, 0).start()
    for sd in (0, 1):
        t_site = (ls, rs)[sd]

        @pl.when(owner & (side == sd))
        def _():
            def rows(slot, c):
                pltpu.make_async_copy(
                    t_site.at[0, pl.ds(row_of(slot), 16)], a2f.at[slot], a2sem.at[slot]
                ).start()
                a2_copy(t_site, slot).start()
                return c

            lax.fori_loop(0, 16, rows, 0)

    def pass_on(i, k):
        x_wait(col_of(i), 4 * k, 4, k)
        to_row(col_of(i), 4 * k, 4).start()

    def start_far():
        for sd in (0, 1):

            @pl.when(hops(sd) == 2)
            def _():
                pieces(sd)

    pass_on(1, 0)

    pltpu.make_async_copy(mpo, mpo, mposem).wait()
    small = split(mpo[...].reshape(256, 16))
    row = lax.broadcasted_iota(jnp.int32, (256, 256), 0)
    col = lax.broadcasted_iota(jnp.int32, (256, 256), 1)
    diagonal = ((row >> 2) & 3) == (col >> 6)

    def ones(mask):
        return jnp.where(mask, 1.0, 0.0).astype(BF16)

    @pl.when(side == 0)
    def _():
        pick = ones((lax.broadcasted_iota(jnp.int32, (256, 16), 0) >> 4)
                    == lax.broadcasted_iota(jnp.int32, (256, 16), 1))
        move = ones(((row >> 4) == (col & 15)) & ((row & 3) == ((col >> 4) & 3)))
        for value, ref in zip(small, (bdh, bdl)):
            wide = lax.dot_general(pick, value, (((1,), (1,)), ((), ())), preferred_element_type=F32)
            wide = jnp.where(((col >> 2) & 3) == (row & 3), wide, 0.0).astype(BF16)
            out = jnp.dot(wide, move, preferred_element_type=F32)
            ref[...] = jnp.where(diagonal, out, 0.0).astype(BF16)

    @pl.when(side == 1)
    def _():
        pick = ones((lax.broadcasted_iota(jnp.int32, (16, 256), 1) & 15)
                    == lax.broadcasted_iota(jnp.int32, (16, 256), 0))
        move = ones(((col >> 4) == (row >> 4)) & (((col >> 2) & 3) == (row & 3)))
        for value, ref in zip(small, (bdh, bdl)):
            wide = jnp.dot(value, pick, preferred_element_type=F32)
            wide = jnp.where((row & 3) == ((col >> 4) & 3), wide, 0.0).astype(BF16)
            out = jnp.dot(move, wide, preferred_element_type=F32)
            ref[...] = jnp.where(diagonal, out, 0.0).astype(BF16)

    pass_on(1, 1)
    for t in range(4):
        pltpu.make_async_copy(a1f.at[t], a1f.at[t], a1sem.at[t]).wait()
        a1h[:, 128 * t : 128 * (t + 1)], a1l[:, 128 * t : 128 * (t + 1)] = split(a1f[t])

    pass_on(1, 2)
    pass_on(1, 3)
    start_far()
    to_sib(4 * core + col_of(1), 1).start()
    for k in range(4):
        pass_on(2, k)

    def turn(n, c):
        for k in (0, 1):
            pltpu.make_async_copy(
                a2f.at[2 * n + k], a2f.at[2 * n + k], a2sem.at[2 * n + k]
            ).wait()
        rows = jnp.concatenate([a2f[2 * n].reshape(64, 512), a2f[2 * n + 1].reshape(64, 512)], axis=0)
        high, low = split(jnp.transpose(rows))
        a2h[:, pl.ds(pl.multiple_of(128 * n, 128), 128)] = high
        a2l[:, pl.ds(pl.multiple_of(128 * n, 128), 128)] = low
        return c

    def first_two(slot):
        lh, ll = split(buf[slot].reshape(256, 512))
        ph, pw = split(dot3(lh, ll, a1h[...], a1l[...]))

        def stack(p):
            return jnp.concatenate(
                [
                    jnp.concatenate(
                        [
                            p[64 * g + 16 * j : 64 * g + 16 * j + 16, 128 * t : 128 * t + 128]
                            for j in range(4)
                            for t in range(4)
                        ],
                        axis=0,
                    )
                    for g in range(4)
                ],
                axis=1,
            )

        oh, ol = split(dot3(bdh[...], bdl[...], stack(ph), stack(pw)))
        for g in range(4):
            at = pl.ds(pl.multiple_of(64 * slot + 16 * g, 16), 16)
            for v in range(16):
                rows, cols = slice(16 * v, 16 * v + 16), slice(128 * g, 128 * g + 128)
                qh[at, 128 * v : 128 * v + 128] = oh[rows, cols]
                ql[at, 128 * v : 128 * v + 128] = ol[rows, cols]

    def step(n, c):
        kind = n % 4
        i = n // 4 - (kind + 1) // 2

        @pl.when((i >= 0) & (i < 4))
        def _():
            xx = col_of(i)
            from_sib = kind // 2
            grp = (1 - from_sib) * (core + 2 * kind) + from_sib * (sib + 2 * (kind - 2))
            slot = 4 * grp + xx

            @pl.when((kind == 0) & (i == 3))
            def _():
                for k in range(4):
                    pass_on(3, k)

            @pl.when(kind > 0)
            def _():
                block_wait(slot)

            @pl.when((kind == 1) | ((kind == 0) & (i > 1)))
            def _():
                to_sib(slot, 4 * kind + i).start()

            first_two(slot)

        @pl.when(n == 0)
        def _():
            lax.fori_loop(0, 8, turn, 0)

        return c

    lax.fori_loop(0, 24, step, 0)

    def last(n, row):
        lhs = pl.ds(pl.multiple_of(128 * row, 128), 128)
        flat = part.reshape(4, 2048, 128)

        def cols(i, c):
            at = pl.ds(pl.multiple_of(256 * i, 256), 256)
            out = dot3(a2h[lhs, :], a2l[lhs, :], qh[:, at], ql[:, at])
            for k in (0, 1):
                flat[n, pl.ds(2 * i + k, 128, stride=16), :] = out[:, 128 * k : 128 * k + 128]
            return c

        lax.fori_loop(0, 8, cols, 0)

    def part_copy(n, row, i):
        at = pl.ds(32 * end_of(i), 32)
        return pltpu.make_async_remote_copy(
            src_ref=part.at[n, at], dst_ref=rcv.at[n, at],
            send_sem=psnd.at[n, i], recv_sem=prcv.at[n, i],
            device_id=dev(z, core, row, x), device_id_type=MESH,
        )

    def end_of(i):
        return (x + 2 + i + i // 2 - 2 * (i // 3)) % 4

    pl.semaphore_wait(near, 7)
    targets = (far, up, down)
    for n, row in enumerate(targets):
        last(n, row)
        for i in range(4):
            part_copy(n, row, i).start()
    last(3, y)

    segment = 2 * z + x % 2
    target = segment + 1 - 2 * side
    valid = (target >= 0) & (target < 8)

    def out_copy(sd, n, xx):
        src = (part.at[3], rcv.at[1])[n]
        half = (y % 2) if n == 0 else 1 - y % 2
        lanes = pl.ds(pl.multiple_of(256 * half + 128 * core, 128), 128)
        out = (nl, nr)[sd]
        return pltpu.make_async_remote_copy(
            src_ref=src.at[pl.ds(32 * xx, 32)], dst_ref=out.at[0, :, :, lanes],
            send_sem=osnd.at[4 * n + xx], recv_sem=orcv.at[4 * sd + 2 * n + core],
            device_id=(target, 4 * y + xx), device_id_type=MESH,
        )

    def out_local(sd, n):
        src = (part.at[3], rcv.at[1])[n]
        half = (y % 2) if n == 0 else 1 - y % 2
        lanes = pl.ds(pl.multiple_of(256 * half + 128 * core, 128), 128)
        out = (nl, nr)[sd]
        return pltpu.make_async_copy(
            src.at[pl.ds(32 * x, 32)], out.at[0, :, :, lanes], orcv.at[4 * sd + 2 * n + core]
        )

    def hand_off(n, xx, wait):
        local = (xx == x) & (target == site)
        for sd in (0, 1):

            @pl.when(valid & (side == sd))
            def _():
                @pl.when(jnp.logical_not(local))
                def _():
                    if wait:
                        out_copy(sd, n, xx).wait_send()
                    else:
                        out_copy(sd, n, xx).start()

                if not wait:

                    @pl.when(local)
                    def _():
                        out_local(sd, n).start()

    for sd in (0, 1):

        @pl.when(keeps[sd])
        def _():
            pltpu.make_async_copy((le, re)[sd].at[0], kept, ksem).wait()
            pltpu.make_async_copy(kept, (nl, nr)[sd].at[0], ksem).start()

    def finish(n, xx):
        def add(k, c):
            at = pl.ds(32 * xx + 8 * k, 8)
            if n == 0:
                part[3, at] = part[3, at] + rcv[0, at]
            else:
                rcv[1, at] = rcv[1, at] + rcv[2, at]
            return c

        lax.fori_loop(0, 4, add, 0)
        hand_off(n, xx, False)

    for i in range(4):
        part_copy(0, far, i).wait_recv()
        finish(0, end_of(i))
    for i in range(4):
        part_copy(1, up, i).wait_recv()
        part_copy(2, down, i).wait_recv()
        finish(1, end_of(i))

    for sd in (0, 1):
        for h in (0, 1):

            @pl.when((hops(sd) != 0) | (core != h))
            def _():
                x_copy(sd, h, 0, 16, 0).wait_send()

    for i in range(4):
        to_row(col_of(i), 0, 16).wait_send()
        to_sib(4 * core + col_of(i), i).wait_send()
        to_sib(8 + 4 * core + col_of(i), 4 + i).wait_send()
    for sd in (0, 1):
        t_site = (ls, rs)[sd]

        @pl.when(owner & (side == sd))
        def _():
            for t in range(4):
                a1_copy(t_site, t).wait_send()
            mpo_copy(sd).wait_send()

            def rows(slot, c):
                a2_copy(t_site, slot).wait_send()
                return c

            lax.fori_loop(0, 16, rows, 0)

    for n, row in enumerate(targets):
        for i in range(4):
            part_copy(n, row, i).wait_send()
    for i in range(4):
        for n in (0, 1):
            hand_off(n, end_of(i), True)
    for sd in (0, 1):

        @pl.when((site > 0) if sd == 0 else (site < 7))
        def _():
            out = (nl, nr)[sd]
            for k in range(4):
                block = out.at[0, :, :, pl.ds(128 * k, 128)]
                pltpu.make_async_copy(block, block, orcv.at[4 * sd + k]).wait()

        @pl.when(keeps[sd])
        def _():
            pltpu.make_async_copy(kept, (nl, nr)[sd].at[0], ksem).wait()


def grow(left_env, right_env, left_site, right_site, left_mpo, right_mpo):
    any_space = pl.BlockSpec(memory_space=pl.ANY)
    dma = pltpu.SemaphoreType.DMA
    vmem = pltpu.VMEM
    return pl.pallas_call(
        kernel,
        out_shape=[jax.ShapeDtypeStruct(left_env.shape, F32)] * 2,
        in_specs=[any_space] * 6,
        out_specs=[any_space] * 2,
        scratch_shapes=[
            vmem((16, 16, 16, 512), F32),
            vmem((4, 512, 128), F32),
            vmem((16, 16, 4, 512), F32),
            vmem((16, 4, 4, 16), F32),
            vmem((512, 512), BF16),
            vmem((512, 512), BF16),
            vmem((512, 1024), BF16),
            vmem((512, 1024), BF16),
            vmem((256, 256), BF16),
            vmem((256, 256), BF16),
            vmem((1024, 2048), BF16),
            vmem((1024, 2048), BF16),
            vmem((4, 128, 16, 128), F32),
            vmem((3, 128, 16, 128), F32),
            vmem((32, 16, 512), F32),
            dma((16,)), dma((4, 4)), dma((4,)), dma((4,)), dma((8,)),
            dma((4,)), dma((16,)), dma, dma((4,)), dma((16,)), dma,
            dma((3, 4)), dma((3, 4)), dma((8,)), dma((8,)), dma,
            pltpu.SemaphoreType.REGULAR,
        ],
        compiler_params=pltpu.CompilerParams(
            collective_id=0, has_side_effects=True, vmem_limit_bytes=62 * 1024 * 1024
        ),
    )(left_env, right_env, left_site, right_site, left_mpo, right_mpo)


def local(left_env, right_env, left_site, right_site, left_mpo, right_mpo):
    def turned(operator):
        return jnp.transpose(operator[0], (0, 2, 3, 1))

    return tuple(
        grow(left_env, right_env, left_site, right_site, turned(left_mpo), turned(right_mpo))
    )


def solution(mesh):
    return jax.shard_map(
        local,
        mesh=mesh,
        in_specs=(
            P("site", "bond", None, None),
            P("site", "bond", None, None),
            P("site", None, None, None),
            P("site", None, None, None),
            P("site", None, None, None, None),
            P("site", None, None, None, None),
        ),
        out_specs=(P("site", "bond", None, None), P("site", "bond", None, None)),
        check_vma=False,
    )
```

```python
import jax
import jax.numpy as jnp
from jax import lax
from jax.experimental import pallas as pl
from jax.experimental.pallas import tpu as pltpu
from jax.sharding import PartitionSpec as P

MESH = pl.DeviceIdType.MESH
F32 = jnp.float32
BF16 = jnp.bfloat16


def split(value):
    high = value.astype(BF16)
    return high, (value - high.astype(F32)).astype(BF16)


def dot3(ah, al, bh, bl):
    out = jnp.dot(ah, bh, preferred_element_type=F32)
    out += jnp.dot(ah, bl, preferred_element_type=F32)
    out += jnp.dot(al, bh, preferred_element_type=F32)
    return out


def kernel(
    le, re, ls, rs, lm, rm, nl, nr,
    buf, a1f, a2f, mpo, a1h, a1l, a2h, a2l, bdh, bdl, qh, ql, part, rcv, kept,
    rsem, xrcv, xsem, ysem, ssem, a1sem, a2sem, mposem, a1snd, a2snd, mposnd,
    prcv, psnd, orcv, osnd, ksem, near,
):
    site = lax.axis_index("site")
    bond = lax.axis_index("bond")
    z, core = site // 2, site % 2
    y, x = bond // 4, bond % 4
    sib = 1 - core
    side = x // 2
    owner = core == x % 2
    e_half = 256 * (y % 2)

    def dev(zz, cc, yy, xx):
        return (2 * zz + cc, 4 * yy + xx)

    up, down, far = (y + 1) % 4, (y + 3) % 4, (y + 2) % 4

    barrier = pltpu.get_barrier_semaphore()

    def greet(n, c):
        there = dev(z, (core + n // 4) % 2, y, (x + n % 4) % 4)
        pl.semaphore_signal(barrier, inc=1, device_id=there, device_id_type=MESH)
        return c

    lax.fori_loop(1, 8, greet, 0)
    for yy in (up, down, far):
        pl.semaphore_signal(barrier, inc=1, device_id=dev(z, core, yy, x), device_id_type=MESH)
    above, below = z < 3, z > 0
    for there, step in ((above, 1), (below, -1)):

        @pl.when(there)
        def _():
            for cc in (0, 1):
                pl.semaphore_signal(
                    barrier, inc=1, device_id=dev(z + step, cc, y, x), device_id_type=MESH
                )

    pl.semaphore_wait(barrier, 10 + 2 * jnp.where(above, 1, 0) + 2 * jnp.where(below, 1, 0))

    def x_copy(sd, h, k):
        return pltpu.make_async_remote_copy(
            src_ref=(le, re)[sd].at[0, pl.ds(16 * h + 2 * k, 2)],
            dst_ref=buf.at[4 * h + k // 2, pl.ds(4 * x + 2 * (k % 2), 2)],
            send_sem=xsem.at[2 * sd + h],
            recv_sem=xrcv.at[x, k],
            device_id=dev(z, h, y, 2 * sd + core),
            device_id_type=MESH,
        )

    def is_local(sd, h):
        return (2 * sd + core == x) & (core == h)

    def x_start(k, c):
        for sd in (0, 1):
            for h in (0, 1):

                @pl.when(is_local(sd, h))
                def _():
                    pltpu.make_async_copy(
                        (le, re)[sd].at[0, pl.ds(16 * h + 2 * k, 2)],
                        buf.at[4 * h + k // 2, pl.ds(4 * x + 2 * (k % 2), 2)],
                        xrcv.at[x, k],
                    ).start()

                @pl.when(jnp.logical_not(is_local(sd, h)))
                def _():
                    x_copy(sd, h, k).start()

        return c

    lax.fori_loop(0, 8, x_start, 0)

    def tell(n, c):
        there = dev(z, (core + n // 4) % 2, y, (x + n % 4) % 4)
        pl.semaphore_signal(near, inc=1, device_id=there, device_id_type=MESH)
        return c

    lax.fori_loop(1, 8, tell, 0)

    keeps = (site == 0, site == 7)
    for sd in (0, 1):

        @pl.when(keeps[sd])
        def _():
            pltpu.make_async_copy((le, re)[sd].at[0], kept, ksem).start()

    def row_of(unit, xx):
        grp, k = unit // 4, unit % 4
        yy = (y + grp // 2 + 2 * (grp // 3)) % 4
        return 128 * yy + 32 * xx + 16 * (grp % 2) + 4 * k

    def a1_src(t_site, t, c):
        return t_site.at[0, :, t, pl.ds(pl.multiple_of(e_half + 128 * c, 128), 128)]

    def a1_copy(t_site, t):
        return pltpu.make_async_remote_copy(
            src_ref=a1_src(t_site, t, sib), dst_ref=a1f.at[t],
            send_sem=a1snd.at[t], recv_sem=a1sem.at[t],
            device_id=dev(z, sib, y, x), device_id_type=MESH,
        )

    def a2_copy(t_site, unit, xx):
        return pltpu.make_async_remote_copy(
            src_ref=t_site.at[0, pl.ds(row_of(unit, xx), 4)],
            dst_ref=a2f.at[unit, pl.ds(4 * xx, 4)],
            send_sem=a2snd.at[unit], recv_sem=a2sem.at[unit],
            device_id=dev(z, sib, y, x), device_id_type=MESH,
        )

    def mpo_copy(sd):
        return pltpu.make_async_remote_copy(
            src_ref=(lm, rm)[sd], dst_ref=mpo, send_sem=mposnd, recv_sem=mposem,
            device_id=dev(z, sib, y, x), device_id_type=MESH,
        )

    for sd in (0, 1):
        t_site = (ls, rs)[sd]

        @pl.when(owner & (side == sd))
        def _():
            for t in range(4):
                pltpu.make_async_copy(a1_src(t_site, t, core), a1f.at[t], a1sem.at[t]).start()
                a1_copy(t_site, t).start()
            pltpu.make_async_copy((lm, rm)[sd], mpo, mposem).start()
            mpo_copy(sd).start()

    def block_wait(slot):
        pltpu.make_async_copy(buf.at[slot], buf.at[slot], rsem.at[slot]).wait()

    def to_sib(slot, n):
        return pltpu.make_async_remote_copy(
            src_ref=buf.at[slot], dst_ref=buf.at[slot],
            send_sem=ssem.at[n], recv_sem=rsem.at[slot],
            device_id=dev(z, sib, y, x), device_id_type=MESH,
        )

    def to_row(xx, k):
        at, unit = pl.ds(4 * xx + 2 * (k % 2), 2), 4 * core + k // 2
        return pltpu.make_async_remote_copy(
            src_ref=buf.at[unit, at], dst_ref=buf.at[8 + unit, at],
            send_sem=ysem.at[k // 2], recv_sem=rsem.at[8 + unit],
            device_id=dev(z, core, (y + 3 + 2 * core) % 4, x), device_id_type=MESH,
        )

    def pass_on(xx, k):
        at = buf.at[4 * core + k // 2, pl.ds(4 * xx + 2 * (k % 2), 2)]
        pltpu.make_async_copy(at, at, xrcv.at[xx, k]).wait()
        to_row(xx, k).start()

    def col_of(i):
        return (x + i + i // 2 - 2 * (i // 3)) % 4

    def own(k, c):
        pass_on(x, k)
        return c

    lax.fori_loop(0, 8, own, 0)
    for sd in (0, 1):
        t_site = (ls, rs)[sd]

        @pl.when(owner & (side == sd))
        def _():
            def rows(n, c):
                unit, xx = n // 4, n % 4
                pltpu.make_async_copy(
                    t_site.at[0, pl.ds(row_of(unit, xx), 4)],
                    a2f.at[unit, pl.ds(4 * xx, 4)],
                    a2sem.at[unit],
                ).start()
                a2_copy(t_site, unit, xx).start()
                return c

            lax.fori_loop(0, 64, rows, 0)

    pltpu.make_async_copy(mpo, mpo, mposem).wait()
    small = split(mpo[...].reshape(256, 16))
    row = lax.broadcasted_iota(jnp.int32, (256, 256), 0)
    col = lax.broadcasted_iota(jnp.int32, (256, 256), 1)
    diagonal = ((row >> 2) & 3) == (col >> 6)

    def ones(mask):
        return jnp.where(mask, 1.0, 0.0).astype(BF16)

    @pl.when(side == 0)
    def _():
        pick = ones((lax.broadcasted_iota(jnp.int32, (256, 16), 0) >> 4)
                    == lax.broadcasted_iota(jnp.int32, (256, 16), 1))
        move = ones(((row >> 4) == (col & 15)) & ((row & 3) == ((col >> 4) & 3)))
        for value, ref in zip(small, (bdh, bdl)):
            wide = lax.dot_general(pick, value, (((1,), (1,)), ((), ())), preferred_element_type=F32)
            wide = jnp.where(((col >> 2) & 3) == (row & 3), wide, 0.0).astype(BF16)
            out = jnp.dot(wide, move, preferred_element_type=F32)
            ref[...] = jnp.where(diagonal, out, 0.0).astype(BF16)

    @pl.when(side == 1)
    def _():
        pick = ones((lax.broadcasted_iota(jnp.int32, (16, 256), 1) & 15)
                    == lax.broadcasted_iota(jnp.int32, (16, 256), 0))
        move = ones(((col >> 4) == (row >> 4)) & (((col >> 2) & 3) == (row & 3)))
        for value, ref in zip(small, (bdh, bdl)):
            wide = jnp.dot(value, pick, preferred_element_type=F32)
            wide = jnp.where((row & 3) == ((col >> 4) & 3), wide, 0.0).astype(BF16)
            out = jnp.dot(move, wide, preferred_element_type=F32)
            ref[...] = jnp.where(diagonal, out, 0.0).astype(BF16)

    for t in range(4):
        pltpu.make_async_copy(a1f.at[t], a1f.at[t], a1sem.at[t]).wait()
        a1h[:, 128 * t : 128 * (t + 1)], a1l[:, 128 * t : 128 * (t + 1)] = split(a1f[t])


    def turn(n, c):
        for k in (0, 1):
            pltpu.make_async_copy(
                a2f.at[2 * n + k], a2f.at[2 * n + k], a2sem.at[2 * n + k]
            ).wait()
        rows = jnp.concatenate([a2f[2 * n].reshape(64, 512), a2f[2 * n + 1].reshape(64, 512)], axis=0)
        high, low = split(jnp.transpose(rows))
        a2h[:, pl.ds(pl.multiple_of(128 * n, 128), 128)] = high
        a2l[:, pl.ds(pl.multiple_of(128 * n, 128), 128)] = low
        return c

    def first_two(slot):
        lh, ll = split(buf[slot].reshape(256, 512))
        ph, pw = split(dot3(lh, ll, a1h[...], a1l[...]))

        def stack(p):
            return jnp.concatenate(
                [
                    jnp.concatenate(
                        [
                            p[64 * g + 16 * j : 64 * g + 16 * j + 16, 128 * t : 128 * t + 128]
                            for j in range(4)
                            for t in range(4)
                        ],
                        axis=0,
                    )
                    for g in range(4)
                ],
                axis=1,
            )

        oh, ol = split(dot3(bdh[...], bdl[...], stack(ph), stack(pw)))
        for g in range(4):
            at = pl.ds(pl.multiple_of(64 * slot + 16 * g, 16), 16)
            for v in range(16):
                rows, cols = slice(16 * v, 16 * v + 16), slice(128 * g, 128 * g + 128)
                qh[at, 128 * v : 128 * v + 128] = oh[rows, cols]
                ql[at, 128 * v : 128 * v + 128] = ol[rows, cols]

    def step(n, c):
        group, kind = n // 4, n % 4
        k = group - 1 + kind // 2
        unit = 4 * (2 - 2 * (kind // 2) + (kind % 2) * sib + (1 - kind % 2) * core) + k

        for i in range(3):

            @pl.when((kind == i) & (group < 4))
            def _():
                for m in (2 * i, 2 * i + 1):
                    pass_on(col_of(m % 3 + 1), 2 * group + m // 3)

        @pl.when((k >= 0) & (k < 4))
        def _():
            @pl.when(kind != 2)
            def _():
                block_wait(unit)

            @pl.when(kind % 2 == 0)
            def _():
                to_sib(unit, 4 * (1 - kind // 2) + k).start()

            first_two(unit)

        @pl.when(n == 3)
        def _():
            lax.fori_loop(0, 8, turn, 0)

        return c

    lax.fori_loop(0, 18, step, 0)

    def last(n, row):
        lhs = pl.ds(pl.multiple_of(128 * row, 128), 128)
        flat = part.reshape(4, 2048, 128)

        def cols(i, c):
            at = pl.ds(pl.multiple_of(256 * i, 256), 256)
            out = dot3(a2h[lhs, :], a2l[lhs, :], qh[:, at], ql[:, at])
            for k in (0, 1):
                flat[n, pl.ds(2 * i + k, 128, stride=16), :] = out[:, 128 * k : 128 * k + 128]
            return c

        lax.fori_loop(0, 8, cols, 0)

    def rows_of(q):
        i = q // 2
        return pl.ds(32 * ((x + 2 + i + i // 2 - 2 * (i // 3)) % 4) + 16 * (q % 2), 16)

    def part_copy(n, row, q):
        at = rows_of(q)
        return pltpu.make_async_remote_copy(
            src_ref=part.at[n, at], dst_ref=rcv.at[n, at],
            send_sem=psnd.at[n, q], recv_sem=prcv.at[n, q],
            device_id=dev(z, core, row, x), device_id_type=MESH,
        )

    pl.semaphore_wait(near, 7)
    targets = (far, up, down)
    for n, row in enumerate(targets):
        last(n, row)

        def send(q, c):
            part_copy(n, row, q).start()
            return c

        lax.fori_loop(0, 8, send, 0)
    last(3, y)

    segment = 2 * z + x % 2
    target = segment + 1 - 2 * side
    valid = (target >= 0) & (target < 8)

    def ends(sd, n, q):
        i = q // 2
        half = (y % 2) if n == 0 else 1 - y % 2
        lanes = pl.ds(pl.multiple_of(256 * half + 128 * core, 128), 128)
        src = (part.at[3], rcv.at[1])[n].at[rows_of(q)]
        dst = (nl, nr)[sd].at[0, pl.ds(16 * (q % 2), 16), :, lanes]
        return src, dst, orcv.at[4 * sd + 2 * n + core], (x + 2 + i + i // 2 - 2 * (i // 3)) % 4

    def out_copy(sd, n, q):
        src, dst, sem, xx = ends(sd, n, q)
        return pltpu.make_async_remote_copy(
            src_ref=src, dst_ref=dst, send_sem=osnd.at[8 * n + q], recv_sem=sem,
            device_id=(target, 4 * y + xx), device_id_type=MESH,
        )

    def hand_off(n, q, wait):
        local = (q // 2 == 3) & (target == site)
        for sd in (0, 1):

            @pl.when(valid & (side == sd))
            def _():
                @pl.when(jnp.logical_not(local))
                def _():
                    if wait:
                        out_copy(sd, n, q).wait_send()
                    else:
                        out_copy(sd, n, q).start()

                if not wait:

                    @pl.when(local)
                    def _():
                        src, dst, sem, _ = ends(sd, n, q)
                        pltpu.make_async_copy(src, dst, sem).start()

    for sd in (0, 1):

        @pl.when(keeps[sd])
        def _():
            pltpu.make_async_copy((le, re)[sd].at[0], kept, ksem).wait()
            pltpu.make_async_copy(kept, (nl, nr)[sd].at[0], ksem).start()

    def finish_far(q, c):
        at = rows_of(q)
        part_copy(0, far, q).wait_recv()
        part[3, at] = part[3, at] + rcv[0, at]
        hand_off(0, q, False)
        return c

    lax.fori_loop(0, 8, finish_far, 0)

    def finish_near(q, c):
        at = rows_of(q)
        part_copy(1, up, q).wait_recv()
        part_copy(2, down, q).wait_recv()
        rcv[1, at] = rcv[1, at] + rcv[2, at]
        hand_off(1, q, False)
        return c

    lax.fori_loop(0, 8, finish_near, 0)

    for sd in (0, 1):
        for h in (0, 1):

            @pl.when(jnp.logical_not(is_local(sd, h)))
            def _():
                pltpu.make_async_remote_copy(
                    src_ref=(le, re)[sd].at[0, pl.ds(16 * h, 16)], dst_ref=buf.at[4 * h],
                    send_sem=xsem.at[2 * sd + h], recv_sem=xrcv.at[x, 0],
                    device_id=dev(z, h, y, 2 * sd + core), device_id_type=MESH,
                ).wait_send()

    for k in range(4):
        pltpu.make_async_remote_copy(
            src_ref=buf.at[4 * core + k], dst_ref=buf.at[8 + 4 * core + k],
            send_sem=ysem.at[k], recv_sem=rsem.at[8 + 4 * core + k],
            device_id=dev(z, core, (y + 3 + 2 * core) % 4, x), device_id_type=MESH,
        ).wait_send()
        to_sib(4 * core + k, k).wait_send()
        to_sib(8 + 4 * core + k, 4 + k).wait_send()
    for sd in (0, 1):
        t_site = (ls, rs)[sd]

        @pl.when(owner & (side == sd))
        def _():
            for t in range(4):
                a1_copy(t_site, t).wait_send()
            mpo_copy(sd).wait_send()

            def rows(unit, c):
                pltpu.make_async_remote_copy(
                    src_ref=t_site.at[0, pl.ds(0, 16)], dst_ref=a2f.at[unit],
                    send_sem=a2snd.at[unit], recv_sem=a2sem.at[unit],
                    device_id=dev(z, sib, y, x), device_id_type=MESH,
                ).wait_send()
                return c

            lax.fori_loop(0, 16, rows, 0)


    def sent(q, c):
        for n, row in enumerate(targets):
            part_copy(n, row, q).wait_send()
        for n in (0, 1):
            hand_off(n, q, True)
        return c

    lax.fori_loop(0, 8, sent, 0)
    for sd in (0, 1):

        @pl.when((site > 0) if sd == 0 else (site < 7))
        def _():
            out = (nl, nr)[sd]
            for k in range(4):
                block = out.at[0, :, :, pl.ds(128 * k, 128)]
                pltpu.make_async_copy(block, block, orcv.at[4 * sd + k]).wait()

        @pl.when(keeps[sd])
        def _():
            pltpu.make_async_copy(kept, (nl, nr)[sd].at[0], ksem).wait()


def grow(left_env, right_env, left_site, right_site, left_mpo, right_mpo):
    any_space = pl.BlockSpec(memory_space=pl.ANY)
    dma = pltpu.SemaphoreType.DMA
    vmem = pltpu.VMEM
    return pl.pallas_call(
        kernel,
        out_shape=[jax.ShapeDtypeStruct(left_env.shape, F32)] * 2,
        in_specs=[any_space] * 6,
        out_specs=[any_space] * 2,
        scratch_shapes=[
            vmem((16, 16, 16, 512), F32),
            vmem((4, 512, 128), F32),
            vmem((16, 16, 4, 512), F32),
            vmem((16, 4, 4, 16), F32),
            vmem((512, 512), BF16),
            vmem((512, 512), BF16),
            vmem((512, 1024), BF16),
            vmem((512, 1024), BF16),
            vmem((256, 256), BF16),
            vmem((256, 256), BF16),
            vmem((1024, 2048), BF16),
            vmem((1024, 2048), BF16),
            vmem((4, 128, 16, 128), F32),
            vmem((3, 128, 16, 128), F32),
            vmem((32, 16, 512), F32),
            dma((16,)), dma((4, 8)), dma((4,)), dma((4,)), dma((8,)),
            dma((4,)), dma((16,)), dma, dma((4,)), dma((16,)), dma,
            dma((3, 8)), dma((3, 8)), dma((8,)), dma((16,)), dma,
            pltpu.SemaphoreType.REGULAR,
        ],
        compiler_params=pltpu.CompilerParams(
            collective_id=0, has_side_effects=True, vmem_limit_bytes=40 * 1024 * 1024
        ),
    )(
        *(
            pltpu.with_memory_space_constraint(array, pltpu.HBM)
            for array in (left_env, right_env, left_site, right_site, left_mpo, right_mpo)
        )
    )


def local(left_env, right_env, left_site, right_site, left_mpo, right_mpo):
    def turned(operator):
        return jnp.transpose(operator[0], (0, 2, 3, 1))

    return tuple(
        grow(left_env, right_env, left_site, right_site, turned(left_mpo), turned(right_mpo))
    )


def solution(mesh):
    return jax.shard_map(
        local,
        mesh=mesh,
        in_specs=(
            P("site", "bond", None, None),
            P("site", "bond", None, None),
            P("site", None, None, None),
            P("site", None, None, None),
            P("site", None, None, None, None),
            P("site", None, None, None, None),
        ),
        out_specs=(P("site", "bond", None, None), P("site", "bond", None, None)),
        check_vma=False,
    )
```

```python
import jax
import jax.numpy as jnp
from jax import lax
from jax.experimental import pallas as pl
from jax.experimental.pallas import tpu as pltpu
from jax.sharding import PartitionSpec as P

MESH = pl.DeviceIdType.MESH
F32 = jnp.float32
BF16 = jnp.bfloat16
AHEAD = 14


def split(value):
    high = value.astype(BF16)
    return high, (value - high.astype(F32)).astype(BF16)


def dot3(ah, al, bh, bl):
    out = jnp.dot(ah, bh, preferred_element_type=F32)
    out += jnp.dot(ah, bl, preferred_element_type=F32)
    out += jnp.dot(al, bh, preferred_element_type=F32)
    return out


def kernel(
    le, re, ls, rs, lm, rm, nl, nr,
    buf, a1f, a2f, mpo, a1h, a1l, a2h, a2l, bdh, bdl, qh, ql, part, rcv, kept,
    rsem, xrcv, xsem, ysem, ssem, a1sem, a2sem, mposem, a1snd, a2snd, mposnd,
    prcv, psnd, orcv, osnd, ksem, near,
):
    site = lax.axis_index("site")
    bond = lax.axis_index("bond")
    z, core = site // 2, site % 2
    y, x = bond // 4, bond % 4
    sib = 1 - core
    side = x // 2
    owner = core == x % 2
    e_half = 256 * (y % 2)

    def dev(zz, cc, yy, xx):
        return (2 * zz + cc, 4 * yy + xx)

    up, down, far = (y + 1) % 4, (y + 3) % 4, (y + 2) % 4

    barrier = pltpu.get_barrier_semaphore()

    def greet(n, c):
        there = dev(z, (core + n // 4) % 2, y, (x + n % 4) % 4)
        pl.semaphore_signal(barrier, inc=1, device_id=there, device_id_type=MESH)
        return c

    lax.fori_loop(1, 8, greet, 0)
    for yy in (up, down, far):
        pl.semaphore_signal(barrier, inc=1, device_id=dev(z, core, yy, x), device_id_type=MESH)
    above, below = z < 3, z > 0
    for there, step in ((above, 1), (below, -1)):

        @pl.when(there)
        def _():
            for cc in (0, 1):
                pl.semaphore_signal(
                    barrier, inc=1, device_id=dev(z + step, cc, y, x), device_id_type=MESH
                )

    pl.semaphore_wait(barrier, 10 + 2 * jnp.where(above, 1, 0) + 2 * jnp.where(below, 1, 0))

    def x_copy(sd, h, k):
        return pltpu.make_async_remote_copy(
            src_ref=(le, re)[sd].at[0, pl.ds(16 * h + 2 * k, 2)],
            dst_ref=buf.at[h + 4 * (k // 2), pl.ds(4 * x + 2 * (k % 2), 2)],
            send_sem=xsem.at[2 * sd + h],
            recv_sem=xrcv.at[x, k],
            device_id=dev(z, h, y, 2 * sd + core),
            device_id_type=MESH,
        )

    def is_local(sd, h):
        return (2 * sd + core == x) & (core == h)

    def x_start(k, c):
        for sd in (0, 1):
            for h in (0, 1):

                @pl.when(is_local(sd, h))
                def _():
                    pltpu.make_async_copy(
                        (le, re)[sd].at[0, pl.ds(16 * h + 2 * k, 2)],
                        buf.at[h + 4 * (k // 2), pl.ds(4 * x + 2 * (k % 2), 2)],
                        xrcv.at[x, k],
                    ).start()

                @pl.when(jnp.logical_not(is_local(sd, h)))
                def _():
                    x_copy(sd, h, k).start()

        return c

    lax.fori_loop(0, 8, x_start, 0)

    def tell(n, c):
        there = dev(z, (core + n // 4) % 2, y, (x + n % 4) % 4)
        pl.semaphore_signal(near, inc=1, device_id=there, device_id_type=MESH)
        return c

    lax.fori_loop(1, 8, tell, 0)

    keeps = (site == 0, site == 7)
    for sd in (0, 1):

        @pl.when(keeps[sd])
        def _():
            pltpu.make_async_copy((le, re)[sd].at[0], kept, ksem).start()

    def row_of(unit, xx):
        grp, k = unit % 4, unit // 4
        yy = (y + grp // 2 + 2 * (grp // 3)) % 4
        return 128 * yy + 32 * xx + 16 * (grp % 2) + 4 * k

    def a1_src(t_site, t, c):
        return t_site.at[0, :, t, pl.ds(pl.multiple_of(e_half + 128 * c, 128), 128)]

    def a1_copy(t_site, t):
        return pltpu.make_async_remote_copy(
            src_ref=a1_src(t_site, t, sib), dst_ref=a1f.at[t],
            send_sem=a1snd.at[t], recv_sem=a1sem.at[t],
            device_id=dev(z, sib, y, x), device_id_type=MESH,
        )

    def a2_copy(t_site, unit, xx):
        return pltpu.make_async_remote_copy(
            src_ref=t_site.at[0, pl.ds(row_of(unit, xx), 4)],
            dst_ref=a2f.at[unit, pl.ds(4 * xx, 4)],
            send_sem=a2snd.at[unit], recv_sem=a2sem.at[unit],
            device_id=dev(z, sib, y, x), device_id_type=MESH,
        )

    def mpo_copy(sd):
        return pltpu.make_async_remote_copy(
            src_ref=(lm, rm)[sd], dst_ref=mpo, send_sem=mposnd, recv_sem=mposem,
            device_id=dev(z, sib, y, x), device_id_type=MESH,
        )

    for sd in (0, 1):
        t_site = (ls, rs)[sd]

        @pl.when(owner & (side == sd))
        def _():
            for t in range(4):
                pltpu.make_async_copy(a1_src(t_site, t, core), a1f.at[t], a1sem.at[t]).start()
                a1_copy(t_site, t).start()
            pltpu.make_async_copy((lm, rm)[sd], mpo, mposem).start()
            mpo_copy(sd).start()

    def block_wait(slot):
        pltpu.make_async_copy(buf.at[slot], buf.at[slot], rsem.at[slot]).wait()

    def to_sib(slot, n):
        return pltpu.make_async_remote_copy(
            src_ref=buf.at[slot], dst_ref=buf.at[slot],
            send_sem=ssem.at[n], recv_sem=rsem.at[slot],
            device_id=dev(z, sib, y, x), device_id_type=MESH,
        )

    def to_row(xx, k):
        at, unit = pl.ds(4 * xx + 2 * (k % 2), 2), core + 4 * (k // 2)
        return pltpu.make_async_remote_copy(
            src_ref=buf.at[unit, at], dst_ref=buf.at[2 + unit, at],
            send_sem=ysem.at[k // 2], recv_sem=rsem.at[2 + unit],
            device_id=dev(z, core, (y + 3 + 2 * core) % 4, x), device_id_type=MESH,
        )

    def pass_on(xx, k):
        at = buf.at[core + 4 * (k // 2), pl.ds(4 * xx + 2 * (k % 2), 2)]
        pltpu.make_async_copy(at, at, xrcv.at[xx, k]).wait()
        to_row(xx, k).start()

    def col_of(i):
        return (x + i + i // 2 - 2 * (i // 3)) % 4

    def own(k, c):
        pass_on(x, k)
        return c

    lax.fori_loop(0, 8, own, 0)
    for sd in (0, 1):
        t_site = (ls, rs)[sd]

        @pl.when(owner & (side == sd))
        def _():
            def rows(n, c):
                unit, xx = n // 4, n % 4
                pltpu.make_async_copy(
                    t_site.at[0, pl.ds(row_of(unit, xx), 4)],
                    a2f.at[unit, pl.ds(4 * xx, 4)],
                    a2sem.at[unit],
                ).start()
                a2_copy(t_site, unit, xx).start()
                return c

            lax.fori_loop(0, 64, rows, 0)

    pltpu.make_async_copy(mpo, mpo, mposem).wait()
    small = split(mpo[...].reshape(256, 16))
    row = lax.broadcasted_iota(jnp.int32, (256, 256), 0)
    col = lax.broadcasted_iota(jnp.int32, (256, 256), 1)
    diagonal = ((row >> 2) & 3) == (col >> 6)

    def ones(mask):
        return jnp.where(mask, 1.0, 0.0).astype(BF16)

    @pl.when(side == 0)
    def _():
        pick = ones((lax.broadcasted_iota(jnp.int32, (256, 16), 0) >> 4)
                    == lax.broadcasted_iota(jnp.int32, (256, 16), 1))
        move = ones(((row >> 4) == (col & 15)) & ((row & 3) == ((col >> 4) & 3)))
        for value, ref in zip(small, (bdh, bdl)):
            wide = lax.dot_general(pick, value, (((1,), (1,)), ((), ())), preferred_element_type=F32)
            wide = jnp.where(((col >> 2) & 3) == (row & 3), wide, 0.0).astype(BF16)
            out = jnp.dot(wide, move, preferred_element_type=F32)
            ref[...] = jnp.where(diagonal, out, 0.0).astype(BF16)

    @pl.when(side == 1)
    def _():
        pick = ones((lax.broadcasted_iota(jnp.int32, (16, 256), 1) & 15)
                    == lax.broadcasted_iota(jnp.int32, (16, 256), 0))
        move = ones(((col >> 4) == (row >> 4)) & (((col >> 2) & 3) == (row & 3)))
        for value, ref in zip(small, (bdh, bdl)):
            wide = jnp.dot(value, pick, preferred_element_type=F32)
            wide = jnp.where((row & 3) == ((col >> 4) & 3), wide, 0.0).astype(BF16)
            out = jnp.dot(move, wide, preferred_element_type=F32)
            ref[...] = jnp.where(diagonal, out, 0.0).astype(BF16)

    for t in range(4):
        pltpu.make_async_copy(a1f.at[t], a1f.at[t], a1sem.at[t]).wait()
        a1h[:, 128 * t : 128 * (t + 1)], a1l[:, 128 * t : 128 * (t + 1)] = split(a1f[t])


    def turn(n, c):
        for k in (0, 1):
            pltpu.make_async_copy(
                a2f.at[2 * n + k], a2f.at[2 * n + k], a2sem.at[2 * n + k]
            ).wait()
        rows = jnp.concatenate([a2f[2 * n].reshape(64, 512), a2f[2 * n + 1].reshape(64, 512)], axis=0)
        high, low = split(jnp.transpose(rows))
        a2h[:, pl.ds(pl.multiple_of(128 * n, 128), 128)] = high
        a2l[:, pl.ds(pl.multiple_of(128 * n, 128), 128)] = low
        return c

    def first_two(slot):
        lh, ll = split(buf[slot].reshape(256, 512))
        ph, pw = split(dot3(lh, ll, a1h[...], a1l[...]))

        def stack(p):
            return jnp.concatenate(
                [
                    jnp.concatenate(
                        [
                            p[64 * g + 16 * j : 64 * g + 16 * j + 16, 128 * t : 128 * t + 128]
                            for j in range(4)
                            for t in range(4)
                        ],
                        axis=0,
                    )
                    for g in range(4)
                ],
                axis=1,
            )

        oh, ol = split(dot3(bdh[...], bdl[...], stack(ph), stack(pw)))
        for g in range(4):
            at = pl.ds(pl.multiple_of(64 * slot + 16 * g, 16), 16)
            for v in range(16):
                rows, cols = slice(16 * v, 16 * v + 16), slice(128 * g, 128 * g + 128)
                qh[at, 128 * v : 128 * v + 128] = oh[rows, cols]
                ql[at, 128 * v : 128 * v + 128] = ol[rows, cols]

    def last(n, row, first, end):
        lhs, deep = pl.ds(pl.multiple_of(128 * row, 128), 128), slice(first, end)
        flat = part.reshape(4, 2048, 128)

        def cols(i, c):
            at = pl.ds(pl.multiple_of(256 * i, 256), 256)
            out = dot3(a2h[lhs, deep], a2l[lhs, deep], qh[deep, at], ql[deep, at])
            for k in (0, 1):
                rows = pl.ds(2 * i + k, 128, stride=16)
                piece = out[:, 128 * k : 128 * k + 128]
                flat[n, rows, :] = piece if first == 0 else flat[n, rows, :] + piece
            return c

        lax.fori_loop(0, 8, cols, 0)

    def step(n, c):
        group, kind = n // 4, n % 4
        k = group - 1 + kind // 2
        unit = 4 * k + 2 - 2 * (kind // 2) + (kind % 2) * sib + (1 - kind % 2) * core

        for i in range(3):

            @pl.when((kind == i) & (group < 4))
            def _():
                for m in (2 * i, 2 * i + 1):
                    pass_on(col_of(m % 3 + 1), 2 * group + m // 3)

        @pl.when((k >= 0) & (k < 4))
        def _():
            @pl.when(kind != 2)
            def _():
                block_wait(unit)

            @pl.when(kind % 2 == 0)
            def _():
                to_sib(unit, 4 * (1 - kind // 2) + k).start()

            first_two(unit)

        @pl.when(n == 3)
        def _():
            lax.fori_loop(0, 8, turn, 0)

        @pl.when(n == AHEAD)
        def _():
            last(0, far, 0, 768)

        return c

    lax.fori_loop(0, 18, step, 0)

    def rows_of(q):
        i = q // 4
        return pl.ds(32 * ((x + 2 + i + i // 2 - 2 * (i // 3)) % 4) + 8 * (q % 4), 8)

    def part_copy(n, row, q):
        at = rows_of(q)
        return pltpu.make_async_remote_copy(
            src_ref=part.at[n, at], dst_ref=rcv.at[n, at],
            send_sem=psnd.at[n, q], recv_sem=prcv.at[n, q],
            device_id=dev(z, core, row, x), device_id_type=MESH,
        )

    pl.semaphore_wait(near, 7)
    targets = (far, up, down)
    for n, row in enumerate(targets):
        last(n, row, 768 if n == 0 else 0, 1024)

        def send(q, c):
            part_copy(n, row, q).start()
            return c

        lax.fori_loop(0, 16, send, 0)
    last(3, y, 0, 1024)

    segment = 2 * z + x % 2
    target = segment + 1 - 2 * side
    valid = (target >= 0) & (target < 8)

    def ends(sd, n, q):
        i = q // 4
        half = (y % 2) if n == 0 else 1 - y % 2
        lanes = pl.ds(pl.multiple_of(256 * half + 128 * core, 128), 128)
        src = (part.at[3], rcv.at[1])[n].at[rows_of(q)]
        dst = (nl, nr)[sd].at[0, pl.ds(8 * (q % 4), 8), :, lanes]
        return src, dst, orcv.at[4 * sd + 2 * n + core], (x + 2 + i + i // 2 - 2 * (i // 3)) % 4

    def out_copy(sd, n, q):
        src, dst, sem, xx = ends(sd, n, q)
        return pltpu.make_async_remote_copy(
            src_ref=src, dst_ref=dst, send_sem=osnd.at[16 * n + q], recv_sem=sem,
            device_id=(target, 4 * y + xx), device_id_type=MESH,
        )

    def hand_off(n, q, wait):
        local = (q // 4 == 3) & (target == site)
        for sd in (0, 1):

            @pl.when(valid & (side == sd))
            def _():
                @pl.when(jnp.logical_not(local))
                def _():
                    if wait:
                        out_copy(sd, n, q).wait_send()
                    else:
                        out_copy(sd, n, q).start()

                if not wait:

                    @pl.when(local)
                    def _():
                        src, dst, sem, _ = ends(sd, n, q)
                        pltpu.make_async_copy(src, dst, sem).start()

    for sd in (0, 1):

        @pl.when(keeps[sd])
        def _():
            pltpu.make_async_copy((le, re)[sd].at[0], kept, ksem).wait()
            pltpu.make_async_copy(kept, (nl, nr)[sd].at[0], ksem).start()

    def finish_far(q, c):
        at = rows_of(q)
        part_copy(0, far, q).wait_recv()
        part[3, at] = part[3, at] + rcv[0, at]
        hand_off(0, q, False)
        return c

    lax.fori_loop(0, 16, finish_far, 0)

    def finish_near(q, c):
        at = rows_of(q)
        part_copy(1, up, q).wait_recv()
        part_copy(2, down, q).wait_recv()
        rcv[1, at] = rcv[1, at] + rcv[2, at]
        hand_off(1, q, False)
        return c

    lax.fori_loop(0, 16, finish_near, 0)

    for sd in (0, 1):
        for h in (0, 1):

            @pl.when(jnp.logical_not(is_local(sd, h)))
            def _():
                pltpu.make_async_remote_copy(
                    src_ref=(le, re)[sd].at[0, pl.ds(16 * h, 16)], dst_ref=buf.at[4 * h],
                    send_sem=xsem.at[2 * sd + h], recv_sem=xrcv.at[x, 0],
                    device_id=dev(z, h, y, 2 * sd + core), device_id_type=MESH,
                ).wait_send()

    for k in range(4):
        pltpu.make_async_remote_copy(
            src_ref=buf.at[4 * k + core], dst_ref=buf.at[4 * k + 2 + core],
            send_sem=ysem.at[k], recv_sem=rsem.at[4 * k + 2 + core],
            device_id=dev(z, core, (y + 3 + 2 * core) % 4, x), device_id_type=MESH,
        ).wait_send()
        to_sib(4 * k + core, k).wait_send()
        to_sib(4 * k + 2 + core, 4 + k).wait_send()
    for sd in (0, 1):
        t_site = (ls, rs)[sd]

        @pl.when(owner & (side == sd))
        def _():
            for t in range(4):
                a1_copy(t_site, t).wait_send()
            mpo_copy(sd).wait_send()

            def rows(unit, c):
                pltpu.make_async_remote_copy(
                    src_ref=t_site.at[0, pl.ds(0, 16)], dst_ref=a2f.at[unit],
                    send_sem=a2snd.at[unit], recv_sem=a2sem.at[unit],
                    device_id=dev(z, sib, y, x), device_id_type=MESH,
                ).wait_send()
                return c

            lax.fori_loop(0, 16, rows, 0)


    def sent(q, c):
        for n, row in enumerate(targets):
            part_copy(n, row, q).wait_send()
        for n in (0, 1):
            hand_off(n, q, True)
        return c

    lax.fori_loop(0, 16, sent, 0)
    for sd in (0, 1):

        @pl.when((site > 0) if sd == 0 else (site < 7))
        def _():
            out = (nl, nr)[sd]
            for k in range(4):
                block = out.at[0, :, :, pl.ds(128 * k, 128)]
                pltpu.make_async_copy(block, block, orcv.at[4 * sd + k]).wait()

        @pl.when(keeps[sd])
        def _():
            pltpu.make_async_copy(kept, (nl, nr)[sd].at[0], ksem).wait()


def grow(left_env, right_env, left_site, right_site, left_mpo, right_mpo):
    any_space = pl.BlockSpec(memory_space=pl.ANY)
    dma = pltpu.SemaphoreType.DMA
    vmem = pltpu.VMEM
    return pl.pallas_call(
        kernel,
        out_shape=[jax.ShapeDtypeStruct(left_env.shape, F32)] * 2,
        in_specs=[any_space] * 6,
        out_specs=[any_space] * 2,
        scratch_shapes=[
            vmem((16, 16, 16, 512), F32),
            vmem((4, 512, 128), F32),
            vmem((16, 16, 4, 512), F32),
            vmem((16, 4, 4, 16), F32),
            vmem((512, 512), BF16),
            vmem((512, 512), BF16),
            vmem((512, 1024), BF16),
            vmem((512, 1024), BF16),
            vmem((256, 256), BF16),
            vmem((256, 256), BF16),
            vmem((1024, 2048), BF16),
            vmem((1024, 2048), BF16),
            vmem((4, 128, 16, 128), F32),
            vmem((3, 128, 16, 128), F32),
            vmem((32, 16, 512), F32),
            dma((16,)), dma((4, 8)), dma((4,)), dma((4,)), dma((8,)),
            dma((4,)), dma((16,)), dma, dma((4,)), dma((16,)), dma,
            dma((3, 16)), dma((3, 16)), dma((8,)), dma((32,)), dma,
            pltpu.SemaphoreType.REGULAR,
        ],
        compiler_params=pltpu.CompilerParams(
            collective_id=0, has_side_effects=True, vmem_limit_bytes=40 * 1024 * 1024
        ),
    )(
        *(
            pltpu.with_memory_space_constraint(array, pltpu.HBM)
            for array in (left_env, right_env, left_site, right_site, left_mpo, right_mpo)
        )
    )


def local(left_env, right_env, left_site, right_site, left_mpo, right_mpo):
    def turned(operator):
        return jnp.transpose(operator[0], (0, 2, 3, 1))

    return tuple(
        grow(left_env, right_env, left_site, right_site, turned(left_mpo), turned(right_mpo))
    )


def solution(mesh):
    return jax.shard_map(
        local,
        mesh=mesh,
        in_specs=(
            P("site", "bond", None, None),
            P("site", "bond", None, None),
            P("site", None, None, None),
            P("site", None, None, None),
            P("site", None, None, None, None),
            P("site", None, None, None, None),
        ),
        out_specs=(P("site", "bond", None, None), P("site", "bond", None, None)),
        check_vma=False,
    )
```

```python
import jax
import jax.numpy as jnp
from jax import lax
from jax.experimental import pallas as pl
from jax.experimental.pallas import tpu as pltpu
from jax.sharding import PartitionSpec as P

MESH = pl.DeviceIdType.MESH
F32 = jnp.float32
BF16 = jnp.bfloat16
AHEAD = 14


def split(value):
    high = value.astype(BF16)
    return high, (value - high.astype(F32)).astype(BF16)


def dot3(ah, al, bh, bl):
    out = jnp.dot(ah, bh, preferred_element_type=F32)
    out += jnp.dot(ah, bl, preferred_element_type=F32)
    out += jnp.dot(al, bh, preferred_element_type=F32)
    return out


def kernel(
    le, re, ls, rs, lm, rm, nl, nr,
    buf, a1f, a2f, mpo, a1h, a1l, a2h, a2l, bdh, bdl, qh, ql, part, rcv, kept,
    rsem, xrcv, xsem, ysem, ssem, a1sem, a2sem, mposem, a1snd, a2snd, mposnd,
    prcv, psnd, orcv, osnd, ksem, near,
):
    site = lax.axis_index("site")
    bond = lax.axis_index("bond")
    z, core = site // 2, site % 2
    y, x = bond // 4, bond % 4
    sib = 1 - core
    side = x // 2
    owner = core == x % 2
    e_half = 256 * (y % 2)

    def dev(zz, cc, yy, xx):
        return (2 * zz + cc, 4 * yy + xx)

    up, down, far = (y + 1) % 4, (y + 3) % 4, (y + 2) % 4

    barrier = pltpu.get_barrier_semaphore()

    def greet(n, c):
        there = dev(z, (core + n // 4) % 2, y, (x + n % 4) % 4)
        pl.semaphore_signal(barrier, inc=1, device_id=there, device_id_type=MESH)
        return c

    lax.fori_loop(1, 8, greet, 0)
    for yy in (up, down, far):
        pl.semaphore_signal(barrier, inc=1, device_id=dev(z, core, yy, x), device_id_type=MESH)
    above, below = z < 3, z > 0
    for there, step in ((above, 1), (below, -1)):

        @pl.when(there)
        def _():
            for cc in (0, 1):
                pl.semaphore_signal(
                    barrier, inc=1, device_id=dev(z + step, cc, y, x), device_id_type=MESH
                )

    pl.semaphore_wait(barrier, 10 + 2 * jnp.where(above, 1, 0) + 2 * jnp.where(below, 1, 0))

    def x_copy(sd, h, k):
        return pltpu.make_async_remote_copy(
            src_ref=(le, re)[sd].at[0, pl.ds(16 * h + 2 * k, 2)],
            dst_ref=buf.at[h + 4 * (k // 2), pl.ds(4 * x + 2 * (k % 2), 2)],
            send_sem=xsem.at[2 * sd + h],
            recv_sem=xrcv.at[x, k],
            device_id=dev(z, h, y, 2 * sd + core),
            device_id_type=MESH,
        )

    def is_local(sd, h):
        return (2 * sd + core == x) & (core == h)

    def x_start(k, c):
        for sd in (0, 1):
            for h in (0, 1):

                @pl.when(is_local(sd, h))
                def _():
                    pltpu.make_async_copy(
                        (le, re)[sd].at[0, pl.ds(16 * h + 2 * k, 2)],
                        buf.at[h + 4 * (k // 2), pl.ds(4 * x + 2 * (k % 2), 2)],
                        xrcv.at[x, k],
                    ).start()

                @pl.when(jnp.logical_not(is_local(sd, h)))
                def _():
                    x_copy(sd, h, k).start()

        return c

    lax.fori_loop(0, 8, x_start, 0)

    def tell(n, c):
        there = dev(z, (core + n // 4) % 2, y, (x + n % 4) % 4)
        pl.semaphore_signal(near, inc=1, device_id=there, device_id_type=MESH)
        return c

    lax.fori_loop(1, 8, tell, 0)

    keeps = (site == 0, site == 7)
    for sd in (0, 1):

        @pl.when(keeps[sd])
        def _():
            pltpu.make_async_copy((le, re)[sd].at[0], kept, ksem).start()

    def row_of(unit, xx):
        grp, k = unit % 4, unit // 4
        yy = (y + grp // 2 + 2 * (grp // 3)) % 4
        return 128 * yy + 32 * xx + 16 * (grp % 2) + 4 * k

    def a1_src(t_site, t, c):
        return t_site.at[0, :, t, pl.ds(pl.multiple_of(e_half + 128 * c, 128), 128)]

    def a1_copy(t_site, t):
        return pltpu.make_async_remote_copy(
            src_ref=a1_src(t_site, t, sib), dst_ref=a1f.at[t],
            send_sem=a1snd.at[t], recv_sem=a1sem.at[t],
            device_id=dev(z, sib, y, x), device_id_type=MESH,
        )

    def a2_copy(t_site, unit, xx):
        return pltpu.make_async_remote_copy(
            src_ref=t_site.at[0, pl.ds(row_of(unit, xx), 4)],
            dst_ref=a2f.at[unit, pl.ds(4 * xx, 4)],
            send_sem=a2snd.at[unit], recv_sem=a2sem.at[unit],
            device_id=dev(z, sib, y, x), device_id_type=MESH,
        )

    def mpo_copy(sd):
        return pltpu.make_async_remote_copy(
            src_ref=(lm, rm)[sd], dst_ref=mpo, send_sem=mposnd, recv_sem=mposem,
            device_id=dev(z, sib, y, x), device_id_type=MESH,
        )

    for sd in (0, 1):
        t_site = (ls, rs)[sd]

        @pl.when(owner & (side == sd))
        def _():
            for t in range(4):
                pltpu.make_async_copy(a1_src(t_site, t, core), a1f.at[t], a1sem.at[t]).start()
                a1_copy(t_site, t).start()
            pltpu.make_async_copy((lm, rm)[sd], mpo, mposem).start()
            mpo_copy(sd).start()

    def block_wait(slot):
        pltpu.make_async_copy(buf.at[slot], buf.at[slot], rsem.at[slot]).wait()

    def to_sib(slot, n):
        return pltpu.make_async_remote_copy(
            src_ref=buf.at[slot], dst_ref=buf.at[slot],
            send_sem=ssem.at[n], recv_sem=rsem.at[slot],
            device_id=dev(z, sib, y, x), device_id_type=MESH,
        )

    def to_row(xx, k):
        at, unit = pl.ds(4 * xx + 2 * (k % 2), 2), core + 4 * (k // 2)
        return pltpu.make_async_remote_copy(
            src_ref=buf.at[unit, at], dst_ref=buf.at[2 + unit, at],
            send_sem=ysem.at[k // 2], recv_sem=rsem.at[2 + unit],
            device_id=dev(z, core, (y + 3 + 2 * core) % 4, x), device_id_type=MESH,
        )

    def pass_on(xx, k):
        at = buf.at[core + 4 * (k // 2), pl.ds(4 * xx + 2 * (k % 2), 2)]
        pltpu.make_async_copy(at, at, xrcv.at[xx, k]).wait()
        to_row(xx, k).start()

    def col_of(i):
        return (x + i + i // 2 - 2 * (i // 3)) % 4

    def own(k, c):
        pass_on(x, k)
        return c

    lax.fori_loop(0, 8, own, 0)
    for sd in (0, 1):
        t_site = (ls, rs)[sd]

        @pl.when(owner & (side == sd))
        def _():
            def rows(n, c):
                unit, xx = n // 4, n % 4
                pltpu.make_async_copy(
                    t_site.at[0, pl.ds(row_of(unit, xx), 4)],
                    a2f.at[unit, pl.ds(4 * xx, 4)],
                    a2sem.at[unit],
                ).start()
                a2_copy(t_site, unit, xx).start()
                return c

            lax.fori_loop(0, 64, rows, 0)

    pltpu.make_async_copy(mpo, mpo, mposem).wait()
    small = split(mpo[...].reshape(256, 16))
    row = lax.broadcasted_iota(jnp.int32, (256, 256), 0)
    col = lax.broadcasted_iota(jnp.int32, (256, 256), 1)
    diagonal = ((row >> 2) & 3) == (col >> 6)

    def ones(mask):
        return jnp.where(mask, 1.0, 0.0).astype(BF16)

    @pl.when(side == 0)
    def _():
        pick = ones((lax.broadcasted_iota(jnp.int32, (256, 16), 0) >> 4)
                    == lax.broadcasted_iota(jnp.int32, (256, 16), 1))
        move = ones(((row >> 4) == (col & 15)) & ((row & 3) == ((col >> 4) & 3)))
        for value, ref in zip(small, (bdh, bdl)):
            wide = lax.dot_general(pick, value, (((1,), (1,)), ((), ())), preferred_element_type=F32)
            wide = jnp.where(((col >> 2) & 3) == (row & 3), wide, 0.0).astype(BF16)
            out = jnp.dot(wide, move, preferred_element_type=F32)
            ref[...] = jnp.where(diagonal, out, 0.0).astype(BF16)

    @pl.when(side == 1)
    def _():
        pick = ones((lax.broadcasted_iota(jnp.int32, (16, 256), 1) & 15)
                    == lax.broadcasted_iota(jnp.int32, (16, 256), 0))
        move = ones(((col >> 4) == (row >> 4)) & (((col >> 2) & 3) == (row & 3)))
        for value, ref in zip(small, (bdh, bdl)):
            wide = jnp.dot(value, pick, preferred_element_type=F32)
            wide = jnp.where((row & 3) == ((col >> 4) & 3), wide, 0.0).astype(BF16)
            out = jnp.dot(move, wide, preferred_element_type=F32)
            ref[...] = jnp.where(diagonal, out, 0.0).astype(BF16)

    for t in range(4):
        pltpu.make_async_copy(a1f.at[t], a1f.at[t], a1sem.at[t]).wait()
        a1h[:, 128 * t : 128 * (t + 1)], a1l[:, 128 * t : 128 * (t + 1)] = split(a1f[t])


    def turn(n, c):
        for k in (0, 1):
            pltpu.make_async_copy(
                a2f.at[2 * n + k], a2f.at[2 * n + k], a2sem.at[2 * n + k]
            ).wait()
        rows = jnp.concatenate([a2f[2 * n].reshape(64, 512), a2f[2 * n + 1].reshape(64, 512)], axis=0)
        high, low = split(jnp.transpose(rows))
        a2h[:, pl.ds(pl.multiple_of(128 * n, 128), 128)] = high
        a2l[:, pl.ds(pl.multiple_of(128 * n, 128), 128)] = low
        return c

    def first_two(slot):
        lh, ll = split(buf[slot].reshape(256, 512))
        ph, pw = split(dot3(lh, ll, a1h[...], a1l[...]))

        def stack(p):
            return jnp.concatenate(
                [
                    jnp.concatenate(
                        [
                            p[64 * g + 16 * j : 64 * g + 16 * j + 16, 128 * t : 128 * t + 128]
                            for j in range(4)
                            for t in range(4)
                        ],
                        axis=0,
                    )
                    for g in range(4)
                ],
                axis=1,
            )

        oh, ol = split(dot3(bdh[...], bdl[...], stack(ph), stack(pw)))
        for g in range(4):
            at = pl.ds(pl.multiple_of(64 * slot + 16 * g, 16), 16)
            for v in range(16):
                rows, cols = slice(16 * v, 16 * v + 16), slice(128 * g, 128 * g + 128)
                qh[at, 128 * v : 128 * v + 128] = oh[rows, cols]
                ql[at, 128 * v : 128 * v + 128] = ol[rows, cols]

    def last(n, row, first, end):
        lhs, deep = pl.ds(pl.multiple_of(128 * row, 128), 128), slice(first, end)
        flat = part.reshape(4, 2048, 128)

        def cols(i, c):
            at = pl.ds(pl.multiple_of(256 * i, 256), 256)
            out = dot3(a2h[lhs, deep], a2l[lhs, deep], qh[deep, at], ql[deep, at])
            for k in (0, 1):
                rows = pl.ds(2 * i + k, 128, stride=16)
                piece = out[:, 128 * k : 128 * k + 128]
                flat[n, rows, :] = piece if first == 0 else flat[n, rows, :] + piece
            return c

        lax.fori_loop(0, 8, cols, 0)

    def step(n, c):
        group, kind = n // 4, n % 4
        k = group - 1 + kind // 2
        unit = 4 * k + 2 - 2 * (kind // 2) + (kind % 2) * sib + (1 - kind % 2) * core

        for i in range(3):

            @pl.when((kind == i) & (group < 4))
            def _():
                for m in (2 * i, 2 * i + 1):
                    pass_on(col_of(m % 3 + 1), 2 * group + m // 3)

        @pl.when((k >= 0) & (k < 4))
        def _():
            @pl.when(kind != 2)
            def _():
                block_wait(unit)

            @pl.when(kind % 2 == 0)
            def _():
                to_sib(unit, 4 * (1 - kind // 2) + k).start()

            first_two(unit)

        @pl.when(n == 3)
        def _():
            lax.fori_loop(0, 8, turn, 0)

        @pl.when(n == AHEAD)
        def _():
            last(0, far, 0, 768)

        return c

    lax.fori_loop(0, 18, step, 0)

    def rows_of(q):
        i = q // 4
        return pl.ds(32 * ((x + 2 + i + i // 2 - 2 * (i // 3)) % 4) + 8 * (q % 4), 8)

    def part_copy(n, row, q):
        at = rows_of(q)
        return pltpu.make_async_remote_copy(
            src_ref=part.at[n, at], dst_ref=rcv.at[n, at],
            send_sem=psnd.at[n], recv_sem=prcv.at[n, q],
            device_id=dev(z, core, row, x), device_id_type=MESH,
        )

    pl.semaphore_wait(near, 7)
    targets = (far, up, down)
    for n, row in enumerate(targets):
        last(n, row, 768 if n == 0 else 0, 1024)

        def send(q, c):
            part_copy(n, row, q).start()
            return c

        lax.fori_loop(0, 16, send, 0)
    last(3, y, 0, 1024)

    segment = 2 * z + x % 2
    target = segment + 1 - 2 * side
    valid = (target >= 0) & (target < 8)

    def ends(sd, n, q):
        i = q // 4
        half = (y % 2) if n == 0 else 1 - y % 2
        lanes = pl.ds(pl.multiple_of(256 * half + 128 * core, 128), 128)
        src = (part.at[3], rcv.at[1])[n].at[rows_of(q)]
        dst = (nl, nr)[sd].at[0, pl.ds(8 * (q % 4), 8), :, lanes]
        return src, dst, orcv.at[4 * sd + 2 * n + core], (x + 2 + i + i // 2 - 2 * (i // 3)) % 4

    def out_copy(sd, n, q):
        src, dst, sem, xx = ends(sd, n, q)
        return pltpu.make_async_remote_copy(
            src_ref=src, dst_ref=dst, send_sem=osnd.at[4 * n + q // 4], recv_sem=sem,
            device_id=(target, 4 * y + xx), device_id_type=MESH,
        )

    def hand_off(n, q):
        local = (q // 4 == 3) & (target == site)
        for sd in (0, 1):

            @pl.when(valid & (side == sd))
            def _():
                @pl.when(jnp.logical_not(local))
                def _():
                    out_copy(sd, n, q).start()

                @pl.when(local)
                def _():
                    src, dst, sem, _ = ends(sd, n, q)
                    pltpu.make_async_copy(src, dst, sem).start()

    for sd in (0, 1):

        @pl.when(keeps[sd])
        def _():
            pltpu.make_async_copy((le, re)[sd].at[0], kept, ksem).wait()
            pltpu.make_async_copy(kept, (nl, nr)[sd].at[0], ksem).start()

    for sd in (0, 1):
        for h in (0, 1):

            @pl.when(jnp.logical_not(is_local(sd, h)))
            def _():
                pltpu.make_async_remote_copy(
                    src_ref=(le, re)[sd].at[0, pl.ds(16 * h, 16)], dst_ref=buf.at[4 * h],
                    send_sem=xsem.at[2 * sd + h], recv_sem=xrcv.at[x, 0],
                    device_id=dev(z, h, y, 2 * sd + core), device_id_type=MESH,
                ).wait_send()

    for k in range(4):
        pltpu.make_async_remote_copy(
            src_ref=buf.at[4 * k + core], dst_ref=buf.at[4 * k + 2 + core],
            send_sem=ysem.at[k], recv_sem=rsem.at[4 * k + 2 + core],
            device_id=dev(z, core, (y + 3 + 2 * core) % 4, x), device_id_type=MESH,
        ).wait_send()
        to_sib(4 * k + core, k).wait_send()
        to_sib(4 * k + 2 + core, 4 + k).wait_send()
    for sd in (0, 1):
        t_site = (ls, rs)[sd]

        @pl.when(owner & (side == sd))
        def _():
            for t in range(4):
                a1_copy(t_site, t).wait_send()
            mpo_copy(sd).wait_send()

            def rows(unit, c):
                pltpu.make_async_remote_copy(
                    src_ref=t_site.at[0, pl.ds(0, 16)], dst_ref=a2f.at[unit],
                    send_sem=a2snd.at[unit], recv_sem=a2sem.at[unit],
                    device_id=dev(z, sib, y, x), device_id_type=MESH,
                ).wait_send()
                return c

            lax.fori_loop(0, 16, rows, 0)

    def finish_far(q, c):
        at = rows_of(q)
        part_copy(0, far, q).wait_recv()
        part[3, at] = part[3, at] + rcv[0, at]
        hand_off(0, q)
        return c

    lax.fori_loop(0, 16, finish_far, 0)

    def finish_near(q, c):
        at = rows_of(q)
        part_copy(1, up, q).wait_recv()
        part_copy(2, down, q).wait_recv()
        rcv[1, at] = rcv[1, at] + rcv[2, at]
        hand_off(1, q)
        return c

    lax.fori_loop(0, 16, finish_near, 0)


    for n, row in enumerate(targets):
        pltpu.make_async_remote_copy(
            src_ref=part.at[n], dst_ref=rcv.at[n], send_sem=psnd.at[n], recv_sem=prcv.at[n, 0],
            device_id=dev(z, core, row, x), device_id_type=MESH,
        ).wait_send()

    for i in range(4):
        for n in (0, 1):

            @pl.when(valid & ((target != site) | (i < 3)))
            def _():
                pltpu.make_async_remote_copy(
                    src_ref=part.at[3, pl.ds(0, 32)], dst_ref=nl.at[0, :, :, pl.ds(0, 128)],
                    send_sem=osnd.at[4 * n + i], recv_sem=orcv.at[0],
                    device_id=dev(z, sib, y, x), device_id_type=MESH,
                ).wait_send()

    for sd in (0, 1):

        @pl.when((site > 0) if sd == 0 else (site < 7))
        def _():
            out = (nl, nr)[sd]
            for k in range(4):
                block = out.at[0, :, :, pl.ds(128 * k, 128)]
                pltpu.make_async_copy(block, block, orcv.at[4 * sd + k]).wait()

        @pl.when(keeps[sd])
        def _():
            pltpu.make_async_copy(kept, (nl, nr)[sd].at[0], ksem).wait()


def grow(left_env, right_env, left_site, right_site, left_mpo, right_mpo):
    any_space = pl.BlockSpec(memory_space=pl.ANY)
    dma = pltpu.SemaphoreType.DMA
    vmem = pltpu.VMEM
    return pl.pallas_call(
        kernel,
        out_shape=[jax.ShapeDtypeStruct(left_env.shape, F32)] * 2,
        in_specs=[any_space] * 6,
        out_specs=[any_space] * 2,
        scratch_shapes=[
            vmem((16, 16, 16, 512), F32),
            vmem((4, 512, 128), F32),
            vmem((16, 16, 4, 512), F32),
            vmem((16, 4, 4, 16), F32),
            vmem((512, 512), BF16),
            vmem((512, 512), BF16),
            vmem((512, 1024), BF16),
            vmem((512, 1024), BF16),
            vmem((256, 256), BF16),
            vmem((256, 256), BF16),
            vmem((1024, 2048), BF16),
            vmem((1024, 2048), BF16),
            vmem((4, 128, 16, 128), F32),
            vmem((3, 128, 16, 128), F32),
            vmem((32, 16, 512), F32),
            dma((16,)), dma((4, 8)), dma((4,)), dma((4,)), dma((8,)),
            dma((4,)), dma((16,)), dma, dma((4,)), dma((16,)), dma,
            dma((3, 16)), dma((3,)), dma((8,)), dma((8,)), dma,
            pltpu.SemaphoreType.REGULAR,
        ],
        compiler_params=pltpu.CompilerParams(
            collective_id=0, has_side_effects=True, vmem_limit_bytes=40 * 1024 * 1024
        ),
    )(
        *(
            pltpu.with_memory_space_constraint(array, pltpu.HBM)
            for array in (left_env, right_env, left_site, right_site, left_mpo, right_mpo)
        )
    )


def local(left_env, right_env, left_site, right_site, left_mpo, right_mpo):
    def turned(operator):
        return jnp.transpose(operator[0], (0, 2, 3, 1))

    return tuple(
        grow(left_env, right_env, left_site, right_site, turned(left_mpo), turned(right_mpo))
    )


def solution(mesh):
    return jax.shard_map(
        local,
        mesh=mesh,
        in_specs=(
            P("site", "bond", None, None),
            P("site", "bond", None, None),
            P("site", None, None, None),
            P("site", None, None, None),
            P("site", None, None, None, None),
            P("site", None, None, None, None),
        ),
        out_specs=(P("site", "bond", None, None), P("site", "bond", None, None)),
        check_vma=False,
    )
```

```python
import jax
import jax.numpy as jnp
from jax import lax
from jax.experimental import pallas as pl
from jax.experimental.pallas import tpu as pltpu
from jax.sharding import PartitionSpec as P

MESH = pl.DeviceIdType.MESH
F32 = jnp.float32
BF16 = jnp.bfloat16
AHEAD = 14


def split(value):
    high = value.astype(BF16)
    return high, (value - high.astype(F32)).astype(BF16)


def dot3(ah, al, bh, bl):
    out = jnp.dot(ah, bh, preferred_element_type=F32)
    out += jnp.dot(ah, bl, preferred_element_type=F32)
    out += jnp.dot(al, bh, preferred_element_type=F32)
    return out


def kernel(
    le, re, ls, rs, lm, rm, nl, nr,
    buf, a1f, a2f, mpo, a1h, a1l, a2h, a2l, bdh, bdl, qh, ql, part, rcv, kept,
    rsem, xrcv, xsem, ysem, ssem, a1sem, a2sem, mposem, a1snd, a2snd, mposnd,
    prcv, psnd, orcv, osnd, ksem, near,
):
    site = lax.axis_index("site")
    bond = lax.axis_index("bond")
    z, core = site // 2, site % 2
    y, x = bond // 4, bond % 4
    sib = 1 - core
    side = x // 2
    owner = core == x % 2
    e_half = 256 * (y % 2)

    def dev(zz, cc, yy, xx):
        return (2 * zz + cc, 4 * yy + xx)

    up, down, far = (y + 1) % 4, (y + 3) % 4, (y + 2) % 4

    barrier = pltpu.get_barrier_semaphore()

    def greet(n, c):
        there = dev(z, (core + n // 4) % 2, y, (x + n % 4) % 4)
        pl.semaphore_signal(barrier, inc=1, device_id=there, device_id_type=MESH)
        return c

    lax.fori_loop(1, 8, greet, 0)
    for yy in (up, down, far):
        pl.semaphore_signal(barrier, inc=1, device_id=dev(z, core, yy, x), device_id_type=MESH)
    above, below = z < 3, z > 0
    for there, step in ((above, 1), (below, -1)):

        @pl.when(there)
        def _():
            for cc in (0, 1):
                pl.semaphore_signal(
                    barrier, inc=1, device_id=dev(z + step, cc, y, x), device_id_type=MESH
                )

    pl.semaphore_wait(barrier, 10 + 2 * jnp.where(above, 1, 0) + 2 * jnp.where(below, 1, 0))

    def x_copy(sd, h, k):
        return pltpu.make_async_remote_copy(
            src_ref=(le, re)[sd].at[0, pl.ds(16 * h + 2 * k, 2)],
            dst_ref=buf.at[h + 4 * (k // 2), pl.ds(4 * x + 2 * (k % 2), 2)],
            send_sem=xsem.at[2 * sd + h],
            recv_sem=xrcv.at[x, k],
            device_id=dev(z, h, y, 2 * sd + core),
            device_id_type=MESH,
        )

    def is_local(sd, h):
        return (2 * sd + core == x) & (core == h)

    def x_start(k, c):
        for sd in (0, 1):
            for h in (0, 1):

                @pl.when(is_local(sd, h))
                def _():
                    pltpu.make_async_copy(
                        (le, re)[sd].at[0, pl.ds(16 * h + 2 * k, 2)],
                        buf.at[h + 4 * (k // 2), pl.ds(4 * x + 2 * (k % 2), 2)],
                        xrcv.at[x, k],
                    ).start()

                @pl.when(jnp.logical_not(is_local(sd, h)))
                def _():
                    x_copy(sd, h, k).start()

        return c

    lax.fori_loop(0, 8, x_start, 0)

    def tell(n, c):
        there = dev(z, (core + n // 4) % 2, y, (x + n % 4) % 4)
        pl.semaphore_signal(near, inc=1, device_id=there, device_id_type=MESH)
        return c

    lax.fori_loop(1, 8, tell, 0)

    keeps = (site == 0, site == 7)
    for sd in (0, 1):

        @pl.when(keeps[sd])
        def _():
            pltpu.make_async_copy((le, re)[sd].at[0], kept, ksem).start()

    def row_of(unit, xx):
        grp, k = unit % 4, unit // 4
        yy = (y + grp // 2 + 2 * (grp // 3)) % 4
        return 128 * yy + 32 * xx + 16 * (grp % 2) + 4 * k

    def a1_src(t_site, t, c):
        return t_site.at[0, :, t, pl.ds(pl.multiple_of(e_half + 128 * c, 128), 128)]

    def a1_copy(t_site, t):
        return pltpu.make_async_remote_copy(
            src_ref=a1_src(t_site, t, sib), dst_ref=a1f.at[t],
            send_sem=a1snd.at[t], recv_sem=a1sem.at[t],
            device_id=dev(z, sib, y, x), device_id_type=MESH,
        )

    def a2_copy(t_site, unit, xx):
        return pltpu.make_async_remote_copy(
            src_ref=t_site.at[0, pl.ds(row_of(unit, xx), 4)],
            dst_ref=a2f.at[unit, pl.ds(4 * xx, 4)],
            send_sem=a2snd.at[unit], recv_sem=a2sem.at[unit],
            device_id=dev(z, sib, y, x), device_id_type=MESH,
        )

    def mpo_copy(sd):
        return pltpu.make_async_remote_copy(
            src_ref=(lm, rm)[sd], dst_ref=mpo, send_sem=mposnd, recv_sem=mposem,
            device_id=dev(z, sib, y, x), device_id_type=MESH,
        )

    for sd in (0, 1):
        t_site = (ls, rs)[sd]

        @pl.when(owner & (side == sd))
        def _():
            for t in range(4):
                pltpu.make_async_copy(a1_src(t_site, t, core), a1f.at[t], a1sem.at[t]).start()
                a1_copy(t_site, t).start()
            pltpu.make_async_copy((lm, rm)[sd], mpo, mposem).start()
            mpo_copy(sd).start()

    def block_wait(slot):
        pltpu.make_async_copy(buf.at[slot], buf.at[slot], rsem.at[slot]).wait()

    def to_sib(slot, n):
        return pltpu.make_async_remote_copy(
            src_ref=buf.at[slot], dst_ref=buf.at[slot],
            send_sem=ssem.at[n], recv_sem=rsem.at[slot],
            device_id=dev(z, sib, y, x), device_id_type=MESH,
        )

    def to_row(xx, k):
        at, unit = pl.ds(4 * xx + 2 * (k % 2), 2), core + 4 * (k // 2)
        return pltpu.make_async_remote_copy(
            src_ref=buf.at[unit, at], dst_ref=buf.at[2 + unit, at],
            send_sem=ysem.at[k // 2], recv_sem=rsem.at[2 + unit],
            device_id=dev(z, core, (y + 3 + 2 * core) % 4, x), device_id_type=MESH,
        )

    def pass_on(xx, k):
        at = buf.at[core + 4 * (k // 2), pl.ds(4 * xx + 2 * (k % 2), 2)]
        pltpu.make_async_copy(at, at, xrcv.at[xx, k]).wait()
        to_row(xx, k).start()

    def col_of(i):
        return (x + i + i // 2 - 2 * (i // 3)) % 4

    def own(k, c):
        pass_on(x, k)
        return c

    lax.fori_loop(0, 8, own, 0)
    for sd in (0, 1):
        t_site = (ls, rs)[sd]

        @pl.when(owner & (side == sd))
        def _():
            def rows(n, c):
                unit, xx = n // 4, n % 4
                pltpu.make_async_copy(
                    t_site.at[0, pl.ds(row_of(unit, xx), 4)],
                    a2f.at[unit, pl.ds(4 * xx, 4)],
                    a2sem.at[unit],
                ).start()
                a2_copy(t_site, unit, xx).start()
                return c

            lax.fori_loop(0, 64, rows, 0)

    pltpu.make_async_copy(mpo, mpo, mposem).wait()
    small = split(mpo[...].reshape(256, 16))
    row = lax.broadcasted_iota(jnp.int32, (256, 256), 0)
    col = lax.broadcasted_iota(jnp.int32, (256, 256), 1)
    diagonal = ((row >> 2) & 3) == (col >> 6)

    def ones(mask):
        return jnp.where(mask, 1.0, 0.0).astype(BF16)

    @pl.when(side == 0)
    def _():
        pick = ones((lax.broadcasted_iota(jnp.int32, (256, 16), 0) >> 4)
                    == lax.broadcasted_iota(jnp.int32, (256, 16), 1))
        move = ones(((row >> 4) == (col & 15)) & ((row & 3) == ((col >> 4) & 3)))
        for value, ref in zip(small, (bdh, bdl)):
            wide = lax.dot_general(pick, value, (((1,), (1,)), ((), ())), preferred_element_type=F32)
            wide = jnp.where(((col >> 2) & 3) == (row & 3), wide, 0.0).astype(BF16)
            out = jnp.dot(wide, move, preferred_element_type=F32)
            ref[...] = jnp.where(diagonal, out, 0.0).astype(BF16)

    @pl.when(side == 1)
    def _():
        pick = ones((lax.broadcasted_iota(jnp.int32, (16, 256), 1) & 15)
                    == lax.broadcasted_iota(jnp.int32, (16, 256), 0))
        move = ones(((col >> 4) == (row >> 4)) & (((col >> 2) & 3) == (row & 3)))
        for value, ref in zip(small, (bdh, bdl)):
            wide = jnp.dot(value, pick, preferred_element_type=F32)
            wide = jnp.where((row & 3) == ((col >> 4) & 3), wide, 0.0).astype(BF16)
            out = jnp.dot(move, wide, preferred_element_type=F32)
            ref[...] = jnp.where(diagonal, out, 0.0).astype(BF16)

    for t in range(4):
        pltpu.make_async_copy(a1f.at[t], a1f.at[t], a1sem.at[t]).wait()
        a1h[:, 128 * t : 128 * (t + 1)], a1l[:, 128 * t : 128 * (t + 1)] = split(a1f[t])


    def turn(n, c):
        for k in (0, 1):
            pltpu.make_async_copy(
                a2f.at[2 * n + k], a2f.at[2 * n + k], a2sem.at[2 * n + k]
            ).wait()
        rows = jnp.concatenate([a2f[2 * n].reshape(64, 512), a2f[2 * n + 1].reshape(64, 512)], axis=0)
        high, low = split(jnp.transpose(rows))
        a2h[:, pl.ds(pl.multiple_of(128 * n, 128), 128)] = high
        a2l[:, pl.ds(pl.multiple_of(128 * n, 128), 128)] = low
        return c

    def first_two(slot):
        lh, ll = split(buf[slot].reshape(256, 512))
        ph, pw = split(dot3(lh, ll, a1h[...], a1l[...]))

        def stack(p):
            return jnp.concatenate(
                [
                    jnp.concatenate(
                        [
                            p[64 * g + 16 * j : 64 * g + 16 * j + 16, 128 * t : 128 * t + 128]
                            for j in range(4)
                            for t in range(4)
                        ],
                        axis=0,
                    )
                    for g in range(4)
                ],
                axis=1,
            )

        oh, ol = split(dot3(bdh[...], bdl[...], stack(ph), stack(pw)))
        for g in range(4):
            at = pl.ds(pl.multiple_of(64 * slot + 16 * g, 16), 16)
            for v in range(16):
                rows, cols = slice(16 * v, 16 * v + 16), slice(128 * g, 128 * g + 128)
                qh[at, 128 * v : 128 * v + 128] = oh[rows, cols]
                ql[at, 128 * v : 128 * v + 128] = ol[rows, cols]

    def last(n, row, first, end):
        lhs, deep = pl.ds(pl.multiple_of(128 * row, 128), 128), slice(first, end)
        flat = part.reshape(4, 2048, 128)

        def cols(i, c):
            at = pl.ds(pl.multiple_of(1024 * i, 1024), 1024)
            out = dot3(a2h[lhs, deep], a2l[lhs, deep], qh[deep, at], ql[deep, at])
            for k in range(8):
                rows = pl.ds(8 * i + k, 128, stride=16)
                piece = out[:, 128 * k : 128 * k + 128]
                flat[n, rows, :] = piece if first == 0 else flat[n, rows, :] + piece
            return c

        lax.fori_loop(0, 2, cols, 0)

    def step(n, c):
        group, kind = n // 4, n % 4
        k = group - 1 + kind // 2
        unit = 4 * k + 2 - 2 * (kind // 2) + (kind % 2) * sib + (1 - kind % 2) * core

        for i in range(3):

            @pl.when((kind == i) & (group < 4))
            def _():
                for m in (2 * i, 2 * i + 1):
                    pass_on(col_of(m % 3 + 1), 2 * group + m // 3)

        @pl.when((k >= 0) & (k < 4))
        def _():
            @pl.when(kind != 2)
            def _():
                block_wait(unit)

            @pl.when(kind % 2 == 0)
            def _():
                to_sib(unit, 4 * (1 - kind // 2) + k).start()

            first_two(unit)

        @pl.when(n == 3)
        def _():
            lax.fori_loop(0, 8, turn, 0)

        @pl.when(n == AHEAD)
        def _():
            last(0, far, 0, 768)

        return c

    lax.fori_loop(0, 18, step, 0)

    def rows_of(q):
        i = q // 4
        return pl.ds(32 * ((x + 2 + i + i // 2 - 2 * (i // 3)) % 4) + 8 * (q % 4), 8)

    def part_copy(n, row, q):
        at = rows_of(q)
        return pltpu.make_async_remote_copy(
            src_ref=part.at[n, at], dst_ref=rcv.at[n, at],
            send_sem=psnd.at[n], recv_sem=prcv.at[n, q],
            device_id=dev(z, core, row, x), device_id_type=MESH,
        )

    pl.semaphore_wait(near, 7)
    targets = (far, up, down)
    for n, row in enumerate(targets):
        last(n, row, 768 if n == 0 else 0, 1024)

        def send(q, c):
            part_copy(n, row, q).start()
            return c

        lax.fori_loop(0, 16, send, 0)
    last(3, y, 0, 1024)

    segment = 2 * z + x % 2
    target = segment + 1 - 2 * side
    valid = (target >= 0) & (target < 8)

    def ends(sd, n, q):
        i = q // 4
        half = (y % 2) if n == 0 else 1 - y % 2
        lanes = pl.ds(pl.multiple_of(256 * half + 128 * core, 128), 128)
        src = (part.at[3], rcv.at[1])[n].at[rows_of(q)]
        dst = (nl, nr)[sd].at[0, pl.ds(8 * (q % 4), 8), :, lanes]
        return src, dst, orcv.at[4 * sd + 2 * n + core], (x + 2 + i + i // 2 - 2 * (i // 3)) % 4

    def out_copy(sd, n, q):
        src, dst, sem, xx = ends(sd, n, q)
        return pltpu.make_async_remote_copy(
            src_ref=src, dst_ref=dst, send_sem=osnd.at[4 * n + q // 4], recv_sem=sem,
            device_id=(target, 4 * y + xx), device_id_type=MESH,
        )

    def hand_off(n, q):
        local = (q // 4 == 3) & (target == site)
        for sd in (0, 1):

            @pl.when(valid & (side == sd))
            def _():
                @pl.when(jnp.logical_not(local))
                def _():
                    out_copy(sd, n, q).start()

                @pl.when(local)
                def _():
                    src, dst, sem, _ = ends(sd, n, q)
                    pltpu.make_async_copy(src, dst, sem).start()

    for sd in (0, 1):

        @pl.when(keeps[sd])
        def _():
            pltpu.make_async_copy((le, re)[sd].at[0], kept, ksem).wait()
            pltpu.make_async_copy(kept, (nl, nr)[sd].at[0], ksem).start()

    for sd in (0, 1):
        for h in (0, 1):

            @pl.when(jnp.logical_not(is_local(sd, h)))
            def _():
                pltpu.make_async_remote_copy(
                    src_ref=(le, re)[sd].at[0, pl.ds(16 * h, 16)], dst_ref=buf.at[4 * h],
                    send_sem=xsem.at[2 * sd + h], recv_sem=xrcv.at[x, 0],
                    device_id=dev(z, h, y, 2 * sd + core), device_id_type=MESH,
                ).wait_send()

    for k in range(4):
        pltpu.make_async_remote_copy(
            src_ref=buf.at[4 * k + core], dst_ref=buf.at[4 * k + 2 + core],
            send_sem=ysem.at[k], recv_sem=rsem.at[4 * k + 2 + core],
            device_id=dev(z, core, (y + 3 + 2 * core) % 4, x), device_id_type=MESH,
        ).wait_send()
        to_sib(4 * k + core, k).wait_send()
        to_sib(4 * k + 2 + core, 4 + k).wait_send()
    for sd in (0, 1):
        t_site = (ls, rs)[sd]

        @pl.when(owner & (side == sd))
        def _():
            for t in range(4):
                a1_copy(t_site, t).wait_send()
            mpo_copy(sd).wait_send()

            def rows(unit, c):
                pltpu.make_async_remote_copy(
                    src_ref=t_site.at[0, pl.ds(0, 16)], dst_ref=a2f.at[unit],
                    send_sem=a2snd.at[unit], recv_sem=a2sem.at[unit],
                    device_id=dev(z, sib, y, x), device_id_type=MESH,
                ).wait_send()
                return c

            lax.fori_loop(0, 16, rows, 0)

    def finish_far(q, c):
        at = rows_of(q)
        part_copy(0, far, q).wait_recv()
        part[3, at] = part[3, at] + rcv[0, at]
        hand_off(0, q)
        return c

    lax.fori_loop(0, 16, finish_far, 0)

    def finish_near(q, c):
        at = rows_of(q)
        part_copy(1, up, q).wait_recv()
        part_copy(2, down, q).wait_recv()
        rcv[1, at] = rcv[1, at] + rcv[2, at]
        hand_off(1, q)
        return c

    lax.fori_loop(0, 16, finish_near, 0)


    for n, row in enumerate(targets):
        pltpu.make_async_remote_copy(
            src_ref=part.at[n], dst_ref=rcv.at[n], send_sem=psnd.at[n], recv_sem=prcv.at[n, 0],
            device_id=dev(z, core, row, x), device_id_type=MESH,
        ).wait_send()

    for i in range(4):
        for n in (0, 1):

            @pl.when(valid & ((target != site) | (i < 3)))
            def _():
                pltpu.make_async_remote_copy(
                    src_ref=part.at[3, pl.ds(0, 32)], dst_ref=nl.at[0, :, :, pl.ds(0, 128)],
                    send_sem=osnd.at[4 * n + i], recv_sem=orcv.at[0],
                    device_id=dev(z, sib, y, x), device_id_type=MESH,
                ).wait_send()

    for sd in (0, 1):

        @pl.when((site > 0) if sd == 0 else (site < 7))
        def _():
            out = (nl, nr)[sd]
            for k in range(4):
                block = out.at[0, :, :, pl.ds(128 * k, 128)]
                pltpu.make_async_copy(block, block, orcv.at[4 * sd + k]).wait()

        @pl.when(keeps[sd])
        def _():
            pltpu.make_async_copy(kept, (nl, nr)[sd].at[0], ksem).wait()


def grow(left_env, right_env, left_site, right_site, left_mpo, right_mpo):
    any_space = pl.BlockSpec(memory_space=pl.ANY)
    dma = pltpu.SemaphoreType.DMA
    vmem = pltpu.VMEM
    return pl.pallas_call(
        kernel,
        out_shape=[jax.ShapeDtypeStruct(left_env.shape, F32)] * 2,
        in_specs=[any_space] * 6,
        out_specs=[any_space] * 2,
        scratch_shapes=[
            vmem((16, 16, 16, 512), F32),
            vmem((4, 512, 128), F32),
            vmem((16, 16, 4, 512), F32),
            vmem((16, 4, 4, 16), F32),
            vmem((512, 512), BF16),
            vmem((512, 512), BF16),
            vmem((512, 1024), BF16),
            vmem((512, 1024), BF16),
            vmem((256, 256), BF16),
            vmem((256, 256), BF16),
            vmem((1024, 2048), BF16),
            vmem((1024, 2048), BF16),
            vmem((4, 128, 16, 128), F32),
            vmem((3, 128, 16, 128), F32),
            vmem((32, 16, 512), F32),
            dma((16,)), dma((4, 8)), dma((4,)), dma((4,)), dma((8,)),
            dma((4,)), dma((16,)), dma, dma((4,)), dma((16,)), dma,
            dma((3, 16)), dma((3,)), dma((8,)), dma((8,)), dma,
            pltpu.SemaphoreType.REGULAR,
        ],
        compiler_params=pltpu.CompilerParams(
            collective_id=0, has_side_effects=True, vmem_limit_bytes=40 * 1024 * 1024
        ),
    )(
        *(
            pltpu.with_memory_space_constraint(array, pltpu.HBM)
            for array in (left_env, right_env, left_site, right_site, left_mpo, right_mpo)
        )
    )


def local(left_env, right_env, left_site, right_site, left_mpo, right_mpo):
    def turned(operator):
        return jnp.transpose(operator[0], (0, 2, 3, 1))

    return tuple(
        grow(left_env, right_env, left_site, right_site, turned(left_mpo), turned(right_mpo))
    )


def solution(mesh):
    return jax.shard_map(
        local,
        mesh=mesh,
        in_specs=(
            P("site", "bond", None, None),
            P("site", "bond", None, None),
            P("site", None, None, None),
            P("site", None, None, None),
            P("site", None, None, None, None),
            P("site", None, None, None, None),
        ),
        out_specs=(P("site", "bond", None, None), P("site", "bond", None, None)),
        check_vma=False,
    )
```

```python
import jax
import jax.numpy as jnp
from jax import lax
from jax.experimental import pallas as pl
from jax.experimental.pallas import tpu as pltpu
from jax.sharding import PartitionSpec as P

MESH = pl.DeviceIdType.MESH
F32 = jnp.float32
BF16 = jnp.bfloat16
AHEAD = 15


def split(value):
    high = value.astype(BF16)
    return high, (value - high.astype(F32)).astype(BF16)


def dot3(ah, al, bh, bl):
    left = jnp.concatenate([ah, ah, al], axis=1)
    right = jnp.concatenate([bh, bl, bh], axis=0)
    return jnp.dot(left, right, preferred_element_type=F32)


def kernel(
    le, re, ls, rs, lm, rm, nl, nr,
    buf, a1f, a2f, mpo, a1h, a1l, a2h, a2l, bdh, bdl, qh, ql, part, rcv, kept,
    rsem, xrcv, xsem, ysem, ssem, a1sem, a2sem, mposem, a1snd, a2snd, mposnd,
    prcv, psnd, orcv, osnd, ksem, near,
):
    site = lax.axis_index("site")
    bond = lax.axis_index("bond")
    z, core = site // 2, site % 2
    y, x = bond // 4, bond % 4
    sib = 1 - core
    side = x // 2
    owner = core == x % 2
    e_half = 256 * (y % 2)

    def dev(zz, cc, yy, xx):
        return (2 * zz + cc, 4 * yy + xx)

    up, down, far = (y + 1) % 4, (y + 3) % 4, (y + 2) % 4

    barrier = pltpu.get_barrier_semaphore()

    def greet(n, c):
        there = dev(z, (core + n // 4) % 2, y, (x + n % 4) % 4)
        pl.semaphore_signal(barrier, inc=1, device_id=there, device_id_type=MESH)
        return c

    lax.fori_loop(1, 8, greet, 0)
    for yy in (up, down, far):
        pl.semaphore_signal(barrier, inc=1, device_id=dev(z, core, yy, x), device_id_type=MESH)
    above, below = z < 3, z > 0
    for there, step in ((above, 1), (below, -1)):

        @pl.when(there)
        def _():
            for cc in (0, 1):
                pl.semaphore_signal(
                    barrier, inc=1, device_id=dev(z + step, cc, y, x), device_id_type=MESH
                )

    pl.semaphore_wait(barrier, 10 + 2 * jnp.where(above, 1, 0) + 2 * jnp.where(below, 1, 0))

    def x_copy(sd, h, k):
        return pltpu.make_async_remote_copy(
            src_ref=(le, re)[sd].at[0, pl.ds(16 * h + 2 * k, 2)],
            dst_ref=buf.at[h + 4 * (k // 2), pl.ds(4 * x + 2 * (k % 2), 2)],
            send_sem=xsem.at[2 * sd + h],
            recv_sem=xrcv.at[x, k],
            device_id=dev(z, h, y, 2 * sd + core),
            device_id_type=MESH,
        )

    def is_local(sd, h):
        return (2 * sd + core == x) & (core == h)

    def x_start(k, c):
        for sd in (0, 1):
            for h in (0, 1):

                @pl.when(is_local(sd, h))
                def _():
                    pltpu.make_async_copy(
                        (le, re)[sd].at[0, pl.ds(16 * h + 2 * k, 2)],
                        buf.at[h + 4 * (k // 2), pl.ds(4 * x + 2 * (k % 2), 2)],
                        xrcv.at[x, k],
                    ).start()

                @pl.when(jnp.logical_not(is_local(sd, h)))
                def _():
                    x_copy(sd, h, k).start()

        return c

    lax.fori_loop(0, 8, x_start, 0)

    def tell(n, c):
        there = dev(z, (core + n // 4) % 2, y, (x + n % 4) % 4)
        pl.semaphore_signal(near, inc=1, device_id=there, device_id_type=MESH)
        return c

    lax.fori_loop(1, 8, tell, 0)

    keeps = (site == 0, site == 7)
    for sd in (0, 1):

        @pl.when(keeps[sd])
        def _():
            pltpu.make_async_copy((le, re)[sd].at[0], kept, ksem).start()

    def row_of(unit, xx):
        grp, k = unit % 4, unit // 4
        yy = (y + grp // 2 + 2 * (grp // 3)) % 4
        return 128 * yy + 32 * xx + 16 * (grp % 2) + 4 * k

    def a1_src(t_site, t, c):
        return t_site.at[0, :, t, pl.ds(pl.multiple_of(e_half + 128 * c, 128), 128)]

    def a1_copy(t_site, t):
        return pltpu.make_async_remote_copy(
            src_ref=a1_src(t_site, t, sib), dst_ref=a1f.at[t],
            send_sem=a1snd.at[t], recv_sem=a1sem.at[t],
            device_id=dev(z, sib, y, x), device_id_type=MESH,
        )

    def a2_copy(t_site, unit, xx):
        return pltpu.make_async_remote_copy(
            src_ref=t_site.at[0, pl.ds(row_of(unit, xx), 4)],
            dst_ref=a2f.at[unit, pl.ds(4 * xx, 4)],
            send_sem=a2snd.at[unit], recv_sem=a2sem.at[unit],
            device_id=dev(z, sib, y, x), device_id_type=MESH,
        )

    def mpo_copy(sd):
        return pltpu.make_async_remote_copy(
            src_ref=(lm, rm)[sd], dst_ref=mpo, send_sem=mposnd, recv_sem=mposem,
            device_id=dev(z, sib, y, x), device_id_type=MESH,
        )

    for sd in (0, 1):
        t_site = (ls, rs)[sd]

        @pl.when(owner & (side == sd))
        def _():
            for t in range(4):
                pltpu.make_async_copy(a1_src(t_site, t, core), a1f.at[t], a1sem.at[t]).start()
                a1_copy(t_site, t).start()
            pltpu.make_async_copy((lm, rm)[sd], mpo, mposem).start()
            mpo_copy(sd).start()

    def block_wait(slot):
        pltpu.make_async_copy(buf.at[slot], buf.at[slot], rsem.at[slot]).wait()

    def to_sib(slot, n):
        return pltpu.make_async_remote_copy(
            src_ref=buf.at[slot], dst_ref=buf.at[slot],
            send_sem=ssem.at[n], recv_sem=rsem.at[slot],
            device_id=dev(z, sib, y, x), device_id_type=MESH,
        )

    def to_row(xx, k):
        at, unit = pl.ds(4 * xx + 2 * (k % 2), 2), core + 4 * (k // 2)
        return pltpu.make_async_remote_copy(
            src_ref=buf.at[unit, at], dst_ref=buf.at[2 + unit, at],
            send_sem=ysem.at[k // 2], recv_sem=rsem.at[2 + unit],
            device_id=dev(z, core, (y + 3 + 2 * core) % 4, x), device_id_type=MESH,
        )

    def pass_on(xx, k):
        at = buf.at[core + 4 * (k // 2), pl.ds(4 * xx + 2 * (k % 2), 2)]
        pltpu.make_async_copy(at, at, xrcv.at[xx, k]).wait()
        to_row(xx, k).start()

    def col_of(i):
        return (x + i + i // 2 - 2 * (i // 3)) % 4

    def own(k, c):
        pass_on(x, k)
        return c

    lax.fori_loop(0, 8, own, 0)
    for sd in (0, 1):
        t_site = (ls, rs)[sd]

        @pl.when(owner & (side == sd))
        def _():
            def rows(n, c):
                unit, xx = n // 4, n % 4
                pltpu.make_async_copy(
                    t_site.at[0, pl.ds(row_of(unit, xx), 4)],
                    a2f.at[unit, pl.ds(4 * xx, 4)],
                    a2sem.at[unit],
                ).start()
                a2_copy(t_site, unit, xx).start()
                return c

            lax.fori_loop(0, 64, rows, 0)

    pltpu.make_async_copy(mpo, mpo, mposem).wait()
    small = split(mpo[...].reshape(256, 16))
    row = lax.broadcasted_iota(jnp.int32, (256, 256), 0)
    col = lax.broadcasted_iota(jnp.int32, (256, 256), 1)
    diagonal = ((row >> 2) & 3) == (col >> 6)

    def ones(mask):
        return jnp.where(mask, 1.0, 0.0).astype(BF16)

    @pl.when(side == 0)
    def _():
        pick = ones((lax.broadcasted_iota(jnp.int32, (256, 16), 0) >> 4)
                    == lax.broadcasted_iota(jnp.int32, (256, 16), 1))
        move = ones(((row >> 4) == (col & 15)) & ((row & 3) == ((col >> 4) & 3)))
        for value, ref in zip(small, (bdh, bdl)):
            wide = lax.dot_general(pick, value, (((1,), (1,)), ((), ())), preferred_element_type=F32)
            wide = jnp.where(((col >> 2) & 3) == (row & 3), wide, 0.0).astype(BF16)
            out = jnp.dot(wide, move, preferred_element_type=F32)
            ref[...] = jnp.where(diagonal, out, 0.0).astype(BF16)

    @pl.when(side == 1)
    def _():
        pick = ones((lax.broadcasted_iota(jnp.int32, (16, 256), 1) & 15)
                    == lax.broadcasted_iota(jnp.int32, (16, 256), 0))
        move = ones(((col >> 4) == (row >> 4)) & (((col >> 2) & 3) == (row & 3)))
        for value, ref in zip(small, (bdh, bdl)):
            wide = jnp.dot(value, pick, preferred_element_type=F32)
            wide = jnp.where((row & 3) == ((col >> 4) & 3), wide, 0.0).astype(BF16)
            out = jnp.dot(move, wide, preferred_element_type=F32)
            ref[...] = jnp.where(diagonal, out, 0.0).astype(BF16)

    for t in range(4):
        pltpu.make_async_copy(a1f.at[t], a1f.at[t], a1sem.at[t]).wait()
        a1h[:, 128 * t : 128 * (t + 1)], a1l[:, 128 * t : 128 * (t + 1)] = split(a1f[t])


    def turn(n, c):
        for k in (0, 1):
            pltpu.make_async_copy(
                a2f.at[2 * n + k], a2f.at[2 * n + k], a2sem.at[2 * n + k]
            ).wait()
        rows = jnp.concatenate([a2f[2 * n].reshape(64, 512), a2f[2 * n + 1].reshape(64, 512)], axis=0)
        high, low = split(jnp.transpose(rows))
        a2h[:, pl.ds(pl.multiple_of(128 * n, 128), 128)] = high
        a2l[:, pl.ds(pl.multiple_of(128 * n, 128), 128)] = low
        return c

    def first_two(slot):
        lh, ll = split(buf[slot].reshape(256, 512))
        ph, pw = split(dot3(lh, ll, a1h[...], a1l[...]))

        def stack(p):
            return jnp.concatenate(
                [
                    jnp.concatenate(
                        [
                            p[64 * g + 16 * j : 64 * g + 16 * j + 16, 128 * t : 128 * t + 128]
                            for j in range(4)
                            for t in range(4)
                        ],
                        axis=0,
                    )
                    for g in range(4)
                ],
                axis=1,
            )

        oh, ol = split(dot3(bdh[...], bdl[...], stack(ph), stack(pw)))
        for g in range(4):
            at = pl.ds(pl.multiple_of(64 * slot + 16 * g, 16), 16)
            for v in range(16):
                rows, cols = slice(16 * v, 16 * v + 16), slice(128 * g, 128 * g + 128)
                qh[at, 128 * v : 128 * v + 128] = oh[rows, cols]
                ql[at, 128 * v : 128 * v + 128] = ol[rows, cols]

    def last(n, row, first, end):
        lhs, deep = pl.ds(pl.multiple_of(128 * row, 128), 128), slice(first, end)
        flat = part.reshape(4, 2048, 128)

        def cols(i, c):
            at = pl.ds(pl.multiple_of(1024 * i, 1024), 1024)
            out = dot3(a2h[lhs, deep], a2l[lhs, deep], qh[deep, at], ql[deep, at])
            for k in range(8):
                rows = pl.ds(8 * i + k, 128, stride=16)
                piece = out[:, 128 * k : 128 * k + 128]
                flat[n, rows, :] = piece if first == 0 else flat[n, rows, :] + piece
            return c

        lax.fori_loop(0, 2, cols, 0)

    def step(n, c):
        group, kind = n // 4, n % 4
        k = group - 1 + kind // 2
        unit = 4 * k + 2 - 2 * (kind // 2) + (kind % 2) * sib + (1 - kind % 2) * core

        for i in range(3):

            @pl.when((kind == i) & (group < 4))
            def _():
                for m in (2 * i, 2 * i + 1):
                    pass_on(col_of(m % 3 + 1), 2 * group + m // 3)

        @pl.when((k >= 0) & (k < 4))
        def _():
            @pl.when(kind != 2)
            def _():
                block_wait(unit)

            @pl.when(kind % 2 == 0)
            def _():
                to_sib(unit, 4 * (1 - kind // 2) + k).start()

            first_two(unit)

        @pl.when(n == 3)
        def _():
            lax.fori_loop(0, 8, turn, 0)

        @pl.when(n == AHEAD)
        def _():
            last(0, far, 0, 768)

        return c

    lax.fori_loop(0, 18, step, 0)

    def rows_of(q):
        i = q // 4
        return pl.ds(32 * ((x + 2 + i + i // 2 - 2 * (i // 3)) % 4) + 8 * (q % 4), 8)

    def part_copy(n, row, q):
        at = rows_of(q)
        return pltpu.make_async_remote_copy(
            src_ref=part.at[n, at], dst_ref=rcv.at[n, at],
            send_sem=psnd.at[n], recv_sem=prcv.at[n, q],
            device_id=dev(z, core, row, x), device_id_type=MESH,
        )

    pl.semaphore_wait(near, 7)
    targets = (far, up, down)
    for n, row in enumerate(targets):
        last(n, row, 768 if n == 0 else 0, 1024)

        def send(q, c):
            part_copy(n, row, q).start()
            return c

        lax.fori_loop(0, 16, send, 0)
    last(3, y, 0, 1024)

    segment = 2 * z + x % 2
    target = segment + 1 - 2 * side
    valid = (target >= 0) & (target < 8)

    def ends(sd, n, q):
        i = q // 4
        half = (y % 2) if n == 0 else 1 - y % 2
        lanes = pl.ds(pl.multiple_of(256 * half + 128 * core, 128), 128)
        src = (part.at[3], rcv.at[1])[n].at[rows_of(q)]
        dst = (nl, nr)[sd].at[0, pl.ds(8 * (q % 4), 8), :, lanes]
        return src, dst, orcv.at[4 * sd + 2 * n + core], (x + 2 + i + i // 2 - 2 * (i // 3)) % 4

    def out_copy(sd, n, q):
        src, dst, sem, xx = ends(sd, n, q)
        return pltpu.make_async_remote_copy(
            src_ref=src, dst_ref=dst, send_sem=osnd.at[4 * n + q // 4], recv_sem=sem,
            device_id=(target, 4 * y + xx), device_id_type=MESH,
        )

    def hand_off(n, q):
        local = (q // 4 == 3) & (target == site)
        for sd in (0, 1):

            @pl.when(valid & (side == sd))
            def _():
                @pl.when(jnp.logical_not(local))
                def _():
                    out_copy(sd, n, q).start()

                @pl.when(local)
                def _():
                    src, dst, sem, _ = ends(sd, n, q)
                    pltpu.make_async_copy(src, dst, sem).start()

    for sd in (0, 1):

        @pl.when(keeps[sd])
        def _():
            pltpu.make_async_copy((le, re)[sd].at[0], kept, ksem).wait()
            pltpu.make_async_copy(kept, (nl, nr)[sd].at[0], ksem).start()

    for sd in (0, 1):
        for h in (0, 1):

            @pl.when(jnp.logical_not(is_local(sd, h)))
            def _():
                pltpu.make_async_remote_copy(
                    src_ref=(le, re)[sd].at[0, pl.ds(16 * h, 16)], dst_ref=buf.at[4 * h],
                    send_sem=xsem.at[2 * sd + h], recv_sem=xrcv.at[x, 0],
                    device_id=dev(z, h, y, 2 * sd + core), device_id_type=MESH,
                ).wait_send()

    for k in range(4):
        pltpu.make_async_remote_copy(
            src_ref=buf.at[4 * k + core], dst_ref=buf.at[4 * k + 2 + core],
            send_sem=ysem.at[k], recv_sem=rsem.at[4 * k + 2 + core],
            device_id=dev(z, core, (y + 3 + 2 * core) % 4, x), device_id_type=MESH,
        ).wait_send()
        to_sib(4 * k + core, k).wait_send()
        to_sib(4 * k + 2 + core, 4 + k).wait_send()
    for sd in (0, 1):
        t_site = (ls, rs)[sd]

        @pl.when(owner & (side == sd))
        def _():
            for t in range(4):
                a1_copy(t_site, t).wait_send()
            mpo_copy(sd).wait_send()

            def rows(unit, c):
                pltpu.make_async_remote_copy(
                    src_ref=t_site.at[0, pl.ds(0, 16)], dst_ref=a2f.at[unit],
                    send_sem=a2snd.at[unit], recv_sem=a2sem.at[unit],
                    device_id=dev(z, sib, y, x), device_id_type=MESH,
                ).wait_send()
                return c

            lax.fori_loop(0, 16, rows, 0)

    def finish_far(q, c):
        at = rows_of(q)
        part_copy(0, far, q).wait_recv()
        part[3, at] = part[3, at] + rcv[0, at]
        hand_off(0, q)
        return c

    lax.fori_loop(0, 16, finish_far, 0)

    def finish_near(q, c):
        at = rows_of(q)
        part_copy(1, up, q).wait_recv()
        part_copy(2, down, q).wait_recv()
        rcv[1, at] = rcv[1, at] + rcv[2, at]
        hand_off(1, q)
        return c

    lax.fori_loop(0, 16, finish_near, 0)


    for n, row in enumerate(targets):
        pltpu.make_async_remote_copy(
            src_ref=part.at[n], dst_ref=rcv.at[n], send_sem=psnd.at[n], recv_sem=prcv.at[n, 0],
            device_id=dev(z, core, row, x), device_id_type=MESH,
        ).wait_send()

    for i in range(4):
        for n in (0, 1):

            @pl.when(valid & ((target != site) | (i < 3)))
            def _():
                pltpu.make_async_remote_copy(
                    src_ref=part.at[3, pl.ds(0, 32)], dst_ref=nl.at[0, :, :, pl.ds(0, 128)],
                    send_sem=osnd.at[4 * n + i], recv_sem=orcv.at[0],
                    device_id=dev(z, sib, y, x), device_id_type=MESH,
                ).wait_send()

    for sd in (0, 1):

        @pl.when((site > 0) if sd == 0 else (site < 7))
        def _():
            out = (nl, nr)[sd]
            for k in range(4):
                block = out.at[0, :, :, pl.ds(128 * k, 128)]
                pltpu.make_async_copy(block, block, orcv.at[4 * sd + k]).wait()

        @pl.when(keeps[sd])
        def _():
            pltpu.make_async_copy(kept, (nl, nr)[sd].at[0], ksem).wait()


def grow(left_env, right_env, left_site, right_site, left_mpo, right_mpo):
    any_space = pl.BlockSpec(memory_space=pl.ANY)
    dma = pltpu.SemaphoreType.DMA
    vmem = pltpu.VMEM
    return pl.pallas_call(
        kernel,
        out_shape=[jax.ShapeDtypeStruct(left_env.shape, F32)] * 2,
        in_specs=[any_space] * 6,
        out_specs=[any_space] * 2,
        scratch_shapes=[
            vmem((16, 16, 16, 512), F32),
            vmem((4, 512, 128), F32),
            vmem((16, 16, 4, 512), F32),
            vmem((16, 4, 4, 16), F32),
            vmem((512, 512), BF16),
            vmem((512, 512), BF16),
            vmem((512, 1024), BF16),
            vmem((512, 1024), BF16),
            vmem((256, 256), BF16),
            vmem((256, 256), BF16),
            vmem((1024, 2048), BF16),
            vmem((1024, 2048), BF16),
            vmem((4, 128, 16, 128), F32),
            vmem((3, 128, 16, 128), F32),
            vmem((32, 16, 512), F32),
            dma((16,)), dma((4, 8)), dma((4,)), dma((4,)), dma((8,)),
            dma((4,)), dma((16,)), dma, dma((4,)), dma((16,)), dma,
            dma((3, 16)), dma((3,)), dma((8,)), dma((8,)), dma,
            pltpu.SemaphoreType.REGULAR,
        ],
        compiler_params=pltpu.CompilerParams(
            collective_id=0, has_side_effects=True, vmem_limit_bytes=40 * 1024 * 1024
        ),
    )(
        *(
            pltpu.with_memory_space_constraint(array, pltpu.HBM)
            for array in (left_env, right_env, left_site, right_site, left_mpo, right_mpo)
        )
    )


def local(left_env, right_env, left_site, right_site, left_mpo, right_mpo):
    def turned(operator):
        return jnp.transpose(operator[0], (0, 2, 3, 1))

    return tuple(
        grow(left_env, right_env, left_site, right_site, turned(left_mpo), turned(right_mpo))
    )


def solution(mesh):
    return jax.shard_map(
        local,
        mesh=mesh,
        in_specs=(
            P("site", "bond", None, None),
            P("site", "bond", None, None),
            P("site", None, None, None),
            P("site", None, None, None),
            P("site", None, None, None, None),
            P("site", None, None, None, None),
        ),
        out_specs=(P("site", "bond", None, None), P("site", "bond", None, None)),
        check_vma=False,
    )
```

```python
import jax
import jax.numpy as jnp
from jax import lax
from jax.experimental import pallas as pl
from jax.experimental.pallas import tpu as pltpu
from jax.sharding import PartitionSpec as P

MESH = pl.DeviceIdType.MESH
F32 = jnp.float32
BF16 = jnp.bfloat16
AHEAD = 15


def split(value):
    high = value.astype(BF16)
    return high, (value - high.astype(F32)).astype(BF16)


def dot3(ah, al, bh, bl):
    out = jnp.dot(ah, bh, preferred_element_type=F32)
    out += jnp.dot(ah, bl, preferred_element_type=F32)
    out += jnp.dot(al, bh, preferred_element_type=F32)
    return out


def kernel(
    le, re, ls, rs, lm, rm, nl, nr,
    buf, a1f, a2f, mpo, a1h, a1l, a2h, a2l, bdh, bdl, qh, ql, part, rcv, kept,
    rsem, xrcv, xsem, ysem, ssem, a1sem, a2sem, mposem, a1snd, a2snd, mposnd,
    prcv, psnd, orcv, osnd, ksem, near,
):
    site = lax.axis_index("site")
    bond = lax.axis_index("bond")
    z, core = site // 2, site % 2
    y, x = bond // 4, bond % 4
    sib = 1 - core
    side = x // 2
    owner = core == x % 2
    e_half = 256 * (y % 2)

    def dev(zz, cc, yy, xx):
        return (2 * zz + cc, 4 * yy + xx)

    up, down, far = (y + 1) % 4, (y + 3) % 4, (y + 2) % 4

    barrier = pltpu.get_barrier_semaphore()

    def greet(n, c):
        there = dev(z, (core + n // 4) % 2, y, (x + n % 4) % 4)
        pl.semaphore_signal(barrier, inc=1, device_id=there, device_id_type=MESH)
        return c

    lax.fori_loop(1, 8, greet, 0)
    for yy in (up, down, far):
        pl.semaphore_signal(barrier, inc=1, device_id=dev(z, core, yy, x), device_id_type=MESH)
    above, below = z < 3, z > 0
    for there, step in ((above, 1), (below, -1)):

        @pl.when(there)
        def _():
            for cc in (0, 1):
                pl.semaphore_signal(
                    barrier, inc=1, device_id=dev(z + step, cc, y, x), device_id_type=MESH
                )

    pl.semaphore_wait(barrier, 10 + 2 * jnp.where(above, 1, 0) + 2 * jnp.where(below, 1, 0))

    def x_copy(sd, h, k):
        return pltpu.make_async_remote_copy(
            src_ref=(le, re)[sd].at[0, pl.ds(16 * h + 2 * k, 2)],
            dst_ref=buf.at[h + 4 * (k // 2), pl.ds(4 * x + 2 * (k % 2), 2)],
            send_sem=xsem.at[2 * sd + h],
            recv_sem=xrcv.at[x, k],
            device_id=dev(z, h, y, 2 * sd + core),
            device_id_type=MESH,
        )

    def is_local(sd, h):
        return (2 * sd + core == x) & (core == h)

    def x_start(k, c):
        for sd in (0, 1):
            for h in (0, 1):

                @pl.when(is_local(sd, h))
                def _():
                    pltpu.make_async_copy(
                        (le, re)[sd].at[0, pl.ds(16 * h + 2 * k, 2)],
                        buf.at[h + 4 * (k // 2), pl.ds(4 * x + 2 * (k % 2), 2)],
                        xrcv.at[x, k],
                    ).start()

                @pl.when(jnp.logical_not(is_local(sd, h)))
                def _():
                    x_copy(sd, h, k).start()

        return c

    lax.fori_loop(0, 8, x_start, 0)

    def tell(n, c):
        there = dev(z, (core + n // 4) % 2, y, (x + n % 4) % 4)
        pl.semaphore_signal(near, inc=1, device_id=there, device_id_type=MESH)
        return c

    lax.fori_loop(1, 8, tell, 0)

    keeps = (site == 0, site == 7)
    for sd in (0, 1):

        @pl.when(keeps[sd])
        def _():
            pltpu.make_async_copy((le, re)[sd].at[0], kept, ksem).start()

    def row_of(unit, xx):
        grp, k = unit % 4, unit // 4
        yy = (y + grp // 2 + 2 * (grp // 3)) % 4
        return 128 * yy + 32 * xx + 16 * (grp % 2) + 4 * k

    def a1_src(t_site, t, c):
        return t_site.at[0, :, t, pl.ds(pl.multiple_of(e_half + 128 * c, 128), 128)]

    def a1_copy(t_site, t):
        return pltpu.make_async_remote_copy(
            src_ref=a1_src(t_site, t, sib), dst_ref=a1f.at[t],
            send_sem=a1snd.at[t], recv_sem=a1sem.at[t],
            device_id=dev(z, sib, y, x), device_id_type=MESH,
        )

    def a2_copy(t_site, unit, xx):
        return pltpu.make_async_remote_copy(
            src_ref=t_site.at[0, pl.ds(row_of(unit, xx), 4)],
            dst_ref=a2f.at[unit, pl.ds(4 * xx, 4)],
            send_sem=a2snd.at[unit], recv_sem=a2sem.at[unit],
            device_id=dev(z, sib, y, x), device_id_type=MESH,
        )

    def mpo_copy(sd):
        return pltpu.make_async_remote_copy(
            src_ref=(lm, rm)[sd], dst_ref=mpo, send_sem=mposnd, recv_sem=mposem,
            device_id=dev(z, sib, y, x), device_id_type=MESH,
        )

    for sd in (0, 1):
        t_site = (ls, rs)[sd]

        @pl.when(owner & (side == sd))
        def _():
            for t in range(4):
                pltpu.make_async_copy(a1_src(t_site, t, core), a1f.at[t], a1sem.at[t]).start()
                a1_copy(t_site, t).start()
            pltpu.make_async_copy((lm, rm)[sd], mpo, mposem).start()
            mpo_copy(sd).start()

    def block_wait(slot):
        pltpu.make_async_copy(buf.at[slot], buf.at[slot], rsem.at[slot]).wait()

    def to_sib(slot, n):
        return pltpu.make_async_remote_copy(
            src_ref=buf.at[slot], dst_ref=buf.at[slot],
            send_sem=ssem.at[n], recv_sem=rsem.at[slot],
            device_id=dev(z, sib, y, x), device_id_type=MESH,
        )

    def to_row(xx, k):
        at, unit = pl.ds(4 * xx + 2 * (k % 2), 2), core + 4 * (k // 2)
        return pltpu.make_async_remote_copy(
            src_ref=buf.at[unit, at], dst_ref=buf.at[2 + unit, at],
            send_sem=ysem.at[k // 2], recv_sem=rsem.at[2 + unit],
            device_id=dev(z, core, (y + 3 + 2 * core) % 4, x), device_id_type=MESH,
        )

    def pass_on(xx, k):
        at = buf.at[core + 4 * (k // 2), pl.ds(4 * xx + 2 * (k % 2), 2)]
        pltpu.make_async_copy(at, at, xrcv.at[xx, k]).wait()
        to_row(xx, k).start()

    def col_of(i):
        return (x + i + i // 2 - 2 * (i // 3)) % 4

    def own(k, c):
        pass_on(x, k)
        return c

    lax.fori_loop(0, 8, own, 0)
    for sd in (0, 1):
        t_site = (ls, rs)[sd]

        @pl.when(owner & (side == sd))
        def _():
            def rows(n, c):
                unit, xx = n // 4, n % 4
                pltpu.make_async_copy(
                    t_site.at[0, pl.ds(row_of(unit, xx), 4)],
                    a2f.at[unit, pl.ds(4 * xx, 4)],
                    a2sem.at[unit],
                ).start()
                a2_copy(t_site, unit, xx).start()
                return c

            lax.fori_loop(0, 64, rows, 0)

    pltpu.make_async_copy(mpo, mpo, mposem).wait()
    small = split(mpo[...].reshape(256, 16))
    row = lax.broadcasted_iota(jnp.int32, (256, 256), 0)
    col = lax.broadcasted_iota(jnp.int32, (256, 256), 1)
    diagonal = ((row >> 2) & 3) == (col >> 6)

    def ones(mask):
        return jnp.where(mask, 1.0, 0.0).astype(BF16)

    @pl.when(side == 0)
    def _():
        pick = ones((lax.broadcasted_iota(jnp.int32, (256, 16), 0) >> 4)
                    == lax.broadcasted_iota(jnp.int32, (256, 16), 1))
        move = ones(((row >> 4) == (col & 15)) & ((row & 3) == ((col >> 4) & 3)))
        for value, ref in zip(small, (bdh, bdl)):
            wide = lax.dot_general(pick, value, (((1,), (1,)), ((), ())), preferred_element_type=F32)
            wide = jnp.where(((col >> 2) & 3) == (row & 3), wide, 0.0).astype(BF16)
            out = jnp.dot(wide, move, preferred_element_type=F32)
            ref[...] = jnp.where(diagonal, out, 0.0).astype(BF16)

    @pl.when(side == 1)
    def _():
        pick = ones((lax.broadcasted_iota(jnp.int32, (16, 256), 1) & 15)
                    == lax.broadcasted_iota(jnp.int32, (16, 256), 0))
        move = ones(((col >> 4) == (row >> 4)) & (((col >> 2) & 3) == (row & 3)))
        for value, ref in zip(small, (bdh, bdl)):
            wide = jnp.dot(value, pick, preferred_element_type=F32)
            wide = jnp.where((row & 3) == ((col >> 4) & 3), wide, 0.0).astype(BF16)
            out = jnp.dot(move, wide, preferred_element_type=F32)
            ref[...] = jnp.where(diagonal, out, 0.0).astype(BF16)

    for t in range(4):
        pltpu.make_async_copy(a1f.at[t], a1f.at[t], a1sem.at[t]).wait()
        a1h[:, 128 * t : 128 * (t + 1)], a1l[:, 128 * t : 128 * (t + 1)] = split(a1f[t])


    def turn(n, c):
        for k in (0, 1):
            pltpu.make_async_copy(
                a2f.at[2 * n + k], a2f.at[2 * n + k], a2sem.at[2 * n + k]
            ).wait()
        rows = jnp.concatenate([a2f[2 * n].reshape(64, 512), a2f[2 * n + 1].reshape(64, 512)], axis=0)
        high, low = split(jnp.transpose(rows))
        a2h[:, pl.ds(pl.multiple_of(128 * n, 128), 128)] = high
        a2l[:, pl.ds(pl.multiple_of(128 * n, 128), 128)] = low
        return c

    def first_two(slot):
        lh, ll = split(buf[slot].reshape(256, 512))
        ph, pw = split(dot3(lh, ll, a1h[...], a1l[...]))

        def stack(p):
            return jnp.concatenate(
                [
                    jnp.concatenate(
                        [
                            p[64 * g + 16 * j : 64 * g + 16 * j + 16, 128 * t : 128 * t + 128]
                            for j in range(4)
                            for t in range(4)
                        ],
                        axis=0,
                    )
                    for g in range(4)
                ],
                axis=1,
            )

        oh, ol = split(dot3(bdh[...], bdl[...], stack(ph), stack(pw)))
        for g in range(4):
            at = pl.ds(pl.multiple_of(64 * slot + 16 * g, 16), 16)
            for v in range(16):
                rows, cols = slice(16 * v, 16 * v + 16), slice(128 * g, 128 * g + 128)
                qh[at, 128 * v : 128 * v + 128] = oh[rows, cols]
                ql[at, 128 * v : 128 * v + 128] = ol[rows, cols]

    def last(n, row, first, end):
        lhs, deep = pl.ds(pl.multiple_of(128 * row, 128), 128), slice(first, end)
        flat = part.reshape(4, 2048, 128)

        def cols(i, c):
            at = pl.ds(pl.multiple_of(1024 * i, 1024), 1024)
            out = dot3(a2h[lhs, deep], a2l[lhs, deep], qh[deep, at], ql[deep, at])
            for k in range(8):
                rows = pl.ds(8 * i + k, 128, stride=16)
                piece = out[:, 128 * k : 128 * k + 128]
                flat[n, rows, :] = piece if first == 0 else flat[n, rows, :] + piece
            return c

        lax.fori_loop(0, 2, cols, 0)

    def step(n, c):
        group, kind = n // 4, n % 4
        k = group - 1 + kind // 2
        unit = 4 * k + 2 - 2 * (kind // 2) + (kind % 2) * sib + (1 - kind % 2) * core

        for i in range(3):

            @pl.when((kind == i) & (group < 4))
            def _():
                for m in (2 * i, 2 * i + 1):
                    pass_on(col_of(m % 3 + 1), 2 * group + m // 3)

        @pl.when((k >= 0) & (k < 4))
        def _():
            @pl.when(kind != 2)
            def _():
                block_wait(unit)

            @pl.when(kind % 2 == 0)
            def _():
                to_sib(unit, 4 * (1 - kind // 2) + k).start()

            first_two(unit)

        @pl.when(n == 3)
        def _():
            lax.fori_loop(0, 8, turn, 0)

        @pl.when(n == AHEAD)
        def _():
            last(0, far, 0, 768)

        return c

    lax.fori_loop(0, 18, step, 0)

    def rows_of(q):
        i = q // 4
        return pl.ds(32 * ((x + 2 + i + i // 2 - 2 * (i // 3)) % 4) + 8 * (q % 4), 8)

    def part_copy(n, row, q):
        at = rows_of(q)
        return pltpu.make_async_remote_copy(
            src_ref=part.at[n, at], dst_ref=rcv.at[n, at],
            send_sem=psnd.at[n], recv_sem=prcv.at[n, q],
            device_id=dev(z, core, row, x), device_id_type=MESH,
        )

    pl.semaphore_wait(near, 7)
    targets = (far, up, down)
    for n, row in enumerate(targets):
        last(n, row, 768 if n == 0 else 0, 1024)

        def send(q, c):
            part_copy(n, row, q).start()
            return c

        lax.fori_loop(0, 16, send, 0)
    last(3, y, 0, 1024)

    segment = 2 * z + x % 2
    target = segment + 1 - 2 * side
    valid = (target >= 0) & (target < 8)

    def ends(sd, n, q):
        i = q // 4
        half = (y % 2) if n == 0 else 1 - y % 2
        lanes = pl.ds(pl.multiple_of(256 * half + 128 * core, 128), 128)
        src = (part.at[3], rcv.at[1])[n].at[rows_of(q)]
        dst = (nl, nr)[sd].at[0, pl.ds(8 * (q % 4), 8), :, lanes]
        return src, dst, orcv.at[4 * sd + 2 * n + core], (x + 2 + i + i // 2 - 2 * (i // 3)) % 4

    def out_copy(sd, n, q):
        src, dst, sem, xx = ends(sd, n, q)
        return pltpu.make_async_remote_copy(
            src_ref=src, dst_ref=dst, send_sem=osnd.at[4 * n + q // 4], recv_sem=sem,
            device_id=(target, 4 * y + xx), device_id_type=MESH,
        )

    def hand_off(n, q):
        local = (q // 4 == 3) & (target == site)
        for sd in (0, 1):

            @pl.when(valid & (side == sd))
            def _():
                @pl.when(jnp.logical_not(local))
                def _():
                    out_copy(sd, n, q).start()

                @pl.when(local)
                def _():
                    src, dst, sem, _ = ends(sd, n, q)
                    pltpu.make_async_copy(src, dst, sem).start()

    for sd in (0, 1):

        @pl.when(keeps[sd])
        def _():
            pltpu.make_async_copy((le, re)[sd].at[0], kept, ksem).wait()
            pltpu.make_async_copy(kept, (nl, nr)[sd].at[0], ksem).start()

    for sd in (0, 1):
        for h in (0, 1):

            @pl.when(jnp.logical_not(is_local(sd, h)))
            def _():
                pltpu.make_async_remote_copy(
                    src_ref=(le, re)[sd].at[0, pl.ds(16 * h, 16)], dst_ref=buf.at[4 * h],
                    send_sem=xsem.at[2 * sd + h], recv_sem=xrcv.at[x, 0],
                    device_id=dev(z, h, y, 2 * sd + core), device_id_type=MESH,
                ).wait_send()

    for k in range(4):
        pltpu.make_async_remote_copy(
            src_ref=buf.at[4 * k + core], dst_ref=buf.at[4 * k + 2 + core],
            send_sem=ysem.at[k], recv_sem=rsem.at[4 * k + 2 + core],
            device_id=dev(z, core, (y + 3 + 2 * core) % 4, x), device_id_type=MESH,
        ).wait_send()
        to_sib(4 * k + core, k).wait_send()
        to_sib(4 * k + 2 + core, 4 + k).wait_send()
    for sd in (0, 1):
        t_site = (ls, rs)[sd]

        @pl.when(owner & (side == sd))
        def _():
            for t in range(4):
                a1_copy(t_site, t).wait_send()
            mpo_copy(sd).wait_send()

            def rows(unit, c):
                pltpu.make_async_remote_copy(
                    src_ref=t_site.at[0, pl.ds(0, 16)], dst_ref=a2f.at[unit],
                    send_sem=a2snd.at[unit], recv_sem=a2sem.at[unit],
                    device_id=dev(z, sib, y, x), device_id_type=MESH,
                ).wait_send()
                return c

            lax.fori_loop(0, 16, rows, 0)

    def finish_far(q, c):
        at = rows_of(q)
        part_copy(0, far, q).wait_recv()
        part[3, at] = part[3, at] + rcv[0, at]
        hand_off(0, q)
        return c

    lax.fori_loop(0, 16, finish_far, 0)

    def finish_near(q, c):
        at = rows_of(q)
        part_copy(1, up, q).wait_recv()
        part_copy(2, down, q).wait_recv()
        rcv[1, at] = rcv[1, at] + rcv[2, at]
        hand_off(1, q)
        return c

    lax.fori_loop(0, 16, finish_near, 0)


    for n, row in enumerate(targets):
        pltpu.make_async_remote_copy(
            src_ref=part.at[n], dst_ref=rcv.at[n], send_sem=psnd.at[n], recv_sem=prcv.at[n, 0],
            device_id=dev(z, core, row, x), device_id_type=MESH,
        ).wait_send()

    for i in range(4):
        for n in (0, 1):

            @pl.when(valid & ((target != site) | (i < 3)))
            def _():
                pltpu.make_async_remote_copy(
                    src_ref=part.at[3, pl.ds(0, 32)], dst_ref=nl.at[0, :, :, pl.ds(0, 128)],
                    send_sem=osnd.at[4 * n + i], recv_sem=orcv.at[0],
                    device_id=dev(z, sib, y, x), device_id_type=MESH,
                ).wait_send()

    for sd in (0, 1):

        @pl.when((site > 0) if sd == 0 else (site < 7))
        def _():
            out = (nl, nr)[sd]
            for k in range(4):
                block = out.at[0, :, :, pl.ds(128 * k, 128)]
                pltpu.make_async_copy(block, block, orcv.at[4 * sd + k]).wait()

        @pl.when(keeps[sd])
        def _():
            pltpu.make_async_copy(kept, (nl, nr)[sd].at[0], ksem).wait()


def grow(left_env, right_env, left_site, right_site, left_mpo, right_mpo):
    any_space = pl.BlockSpec(memory_space=pl.ANY)
    dma = pltpu.SemaphoreType.DMA
    vmem = pltpu.VMEM
    return pl.pallas_call(
        kernel,
        out_shape=[jax.ShapeDtypeStruct(left_env.shape, F32)] * 2,
        in_specs=[any_space] * 6,
        out_specs=[any_space] * 2,
        scratch_shapes=[
            vmem((16, 16, 16, 512), F32),
            vmem((4, 512, 128), F32),
            vmem((16, 16, 4, 512), F32),
            vmem((16, 4, 4, 16), F32),
            vmem((512, 512), BF16),
            vmem((512, 512), BF16),
            vmem((512, 1024), BF16),
            vmem((512, 1024), BF16),
            vmem((256, 256), BF16),
            vmem((256, 256), BF16),
            vmem((1024, 2048), BF16),
            vmem((1024, 2048), BF16),
            vmem((4, 128, 16, 128), F32),
            vmem((3, 128, 16, 128), F32),
            vmem((32, 16, 512), F32),
            dma((16,)), dma((4, 8)), dma((4,)), dma((4,)), dma((8,)),
            dma((4,)), dma((16,)), dma, dma((4,)), dma((16,)), dma,
            dma((3, 16)), dma((3,)), dma((8,)), dma((8,)), dma,
            pltpu.SemaphoreType.REGULAR,
        ],
        compiler_params=pltpu.CompilerParams(
            collective_id=0, has_side_effects=True, vmem_limit_bytes=40 * 1024 * 1024
        ),
    )(
        *(
            pltpu.with_memory_space_constraint(array, pltpu.HBM)
            for array in (left_env, right_env, left_site, right_site, left_mpo, right_mpo)
        )
    )


def local(left_env, right_env, left_site, right_site, left_mpo, right_mpo):
    def turned(operator):
        return jnp.transpose(operator[0], (0, 2, 3, 1))

    return tuple(
        grow(left_env, right_env, left_site, right_site, turned(left_mpo), turned(right_mpo))
    )


def solution(mesh):
    return jax.shard_map(
        local,
        mesh=mesh,
        in_specs=(
            P("site", "bond", None, None),
            P("site", "bond", None, None),
            P("site", None, None, None),
            P("site", None, None, None),
            P("site", None, None, None, None),
            P("site", None, None, None, None),
        ),
        out_specs=(P("site", "bond", None, None), P("site", "bond", None, None)),
        check_vma=False,
    )
```
